32 devices in a mesh: tm: 32 (over z, y, x, core).
Axes of the slice: x: 2, y: 2, z: 4, core: 2. Of those that a mesh axis runs over, the one named last changes fastest.
Arguments:
- initial: float32 [2, 64, 64], replicated, may hold values from 0 to 0.6
- coarse_guess: float32 [32, 2, 64, 64], P('tm'), may hold values from 0 to 0.6
- feed_rate: float32 [64, 64], replicated, may hold values from 0.02 to 0.08
- kill_rate: float32 [64, 64], replicated, may hold values from 0.03 to 0.07
Outputs:
- trajectory: float32 [128, 2, 64, 64], P('tm')
- c_residual: float32 [32, 2, 64, 64], P('tm')
- group_coarse: float32 [32, 2, 64, 64], P('tm')
- level_defect: float32 [32, 2, 64, 64], P('tm')
The draws below stay inside these ranges and needn't reach their ends.
All inputs are finite; a program needn't handle non-finite values.
Results may differ from the reference program's by a relative error of at most 0.0004.
Values sent between devices are 32-bit elements; how exact they have to be, the bound alone decides.
A program may use at most 64 MiB of HBM per device.

```python
import math
import jax
import jax.numpy as jnp
from jax import lax

STEPS_DEV = 4
GX = 64
GY = 64
GROUP = 16
N_TM = 32


def steps_of(stream_key, dims, shards, smallest, top_value):
    def one(position, parts):
        heights = jax.random.uniform(jax.random.fold_in(jax.random.fold_in(stream_key, 6), position), (parts,), jnp.float32, smallest / len(shards), top_value / len(shards))
        return jnp.repeat(jnp.exp(heights), dims[position] // parts).reshape((-1,) + (1,) * (len(dims) - position - 1))

    level = one(*shards[0])
    for cut in shards[1:]:
        level = level * one(*cut)
    return level


def setup_inputs(seed: int = 0) -> dict:
    key_list = jax.random.split(jax.random.key(seed), 5)
    return {
        "initial": jnp.clip(jax.random.uniform(key_list[0], (2, GX, GY), jnp.float32, 0.0, 0.6), 0.0, 0.6),
        "coarse_guess": jnp.clip(0.6 * jax.random.uniform(key_list[1], (N_TM, 2, GX, GY), jnp.float32) ** steps_of(key_list[1], (N_TM, 2, GX, GY), ((0, 32),), -0.2, 0.2), 0.0, 0.6),
        "feed_rate": jnp.clip(jnp.exp(jax.random.uniform(key_list[2], (GX, GY), jnp.float32, math.log(0.02), math.log(0.08))), 0.02, 0.08),
        "kill_rate": jnp.clip(jnp.exp(jax.random.uniform(key_list[3], (GX, GY), jnp.float32, math.log(0.03), math.log(0.07))), 0.03, 0.07),
    }


diffusion = (0.2, 0.1)
interval_time = 0.03125
highest = lax.Precision.HIGHEST

def cosine_basis(length):
    positions = jnp.arange(length, dtype=jnp.float32)
    angles = jnp.pi * (positions[:, None] + 0.5) * positions[None, :] / length
    weight = jnp.where(positions == 0, jnp.sqrt(1.0 / length), jnp.sqrt(2.0 / length))
    return jnp.cos(angles) * weight[None, :]

def eigen_values(length):
    positions = jnp.arange(length, dtype=jnp.float32)
    return -4.0 * jnp.sin(jnp.pi * positions / (2.0 * length)) ** 2

def make_tables(rows_first, rows_second):
    spectrum = eigen_values(rows_first)[:, None] + eigen_values(rows_second)[None, :]
    return (cosine_basis(rows_first), cosine_basis(rows_second), spectrum)

def advance(fields, feed_rate, kill_rate, time_step, tables):
    basis_rows, basis_cols, spectrum = tables
    substrate = fields[..., 0, :, :]
    catalyst = fields[..., 1, :, :]
    uptake = substrate * catalyst * catalyst
    substrate_new = substrate + time_step * (feed_rate * (1.0 - substrate) - uptake)
    catalyst_new = catalyst + time_step * (uptake - (feed_rate + kill_rate) * catalyst)
    reacted = jnp.stack([substrate_new, catalyst_new], axis=-3)
    spectral = jnp.matmul(jnp.matmul(basis_rows.T, reacted, precision=highest), basis_cols, precision=highest)
    diff_rates = jnp.array(diffusion, dtype=jnp.float32)
    spectral = spectral / (1.0 - time_step * diff_rates[:, None, None] * spectrum)
    return jnp.matmul(jnp.matmul(basis_rows, spectral, precision=highest), basis_cols.T, precision=highest)

def march(start_state, feed_rate, kill_rate, time_step, tables, count_steps):

    def turn(fields, unused):
        fields = advance(fields, feed_rate, kill_rate, time_step, tables)
        return (fields, fields)
    finished, visited = lax.scan(turn, start_state, None, length=count_steps)
    return (finished, visited)

def reference(initial, coarse_guess, feed_rate, kill_rate):
    tables = make_tables(initial.shape[1], initial.shape[2])
    fine_step = interval_time / STEPS_DEV
    level_step = interval_time
    coarse_step = interval_time * GROUP
    groups = N_TM // GROUP
    shape = initial.shape

    def before(values):
        return jnp.concatenate([initial[None], values[:-1]], axis=0)

    def evolve(fields, time_step):
        return advance(fields, feed_rate, kill_rate, time_step, tables)
    relaxed, unused = march(before(coarse_guess), feed_rate, kill_rate, fine_step, tables, STEPS_DEV)
    shifted = before(relaxed)
    arrived, unused = march(shifted, feed_rate, kill_rate, fine_step, tables, STEPS_DEV)
    c_residual = arrived - relaxed
    level_rhs = arrived - evolve(shifted, level_step)
    grouped_terms = level_rhs.reshape((groups, GROUP) + shape)
    group_start = jnp.concatenate([initial[None], relaxed.reshape((groups, GROUP) + shape)[:, -1][:-1]], axis=0)

    def level_turn(fields, right_side):
        fields = evolve(fields, level_step) + right_side
        return (fields, fields)
    inner_terms = jnp.moveaxis(grouped_terms[:, :-1], 1, 0)
    last_point, unused = lax.scan(level_turn, group_start, inner_terms)
    closing = evolve(last_point, level_step) + grouped_terms[:, -1]
    coarse_rhs = closing - evolve(group_start, coarse_step)

    def coarse_turn(fields, right_side):
        fields = evolve(fields, coarse_step) + right_side
        return (fields, fields)
    unused, coarse_values = lax.scan(coarse_turn, initial, coarse_rhs)
    group_coarse = jnp.repeat(coarse_values, GROUP, axis=0)
    fresh_start = jnp.concatenate([initial[None], coarse_values[:-1]], axis=0)
    unused, interior = lax.scan(level_turn, fresh_start, inner_terms)
    finishing = evolve(interior[-1], level_step) + grouped_terms[:, -1]
    group_defect = finishing - coarse_values
    level_defect = jnp.concatenate([jnp.zeros((groups, GROUP - 1) + shape, jnp.float32), group_defect[:, None]], axis=1)
    level_defect = level_defect.reshape((N_TM,) + shape)
    corrected = jnp.concatenate([jnp.moveaxis(interior, 0, 1), coarse_values[:, None]], axis=1)
    corrected = corrected.reshape((N_TM,) + shape)
    unused, inside = march(before(corrected), feed_rate, kill_rate, fine_step, tables, STEPS_DEV - 1)
    trajectory = jnp.concatenate([jnp.moveaxis(inside, 0, 1), corrected[:, None]], axis=1)
    return (trajectory.reshape((N_TM * STEPS_DEV,) + shape), c_residual, group_coarse, level_defect)
```

```python
import functools

import jax
import jax.numpy as jnp
import ml_dtypes
import numpy as np
from jax import lax
from jax.experimental import pallas as pl
from jax.experimental.pallas import tpu as pltpu
from jax.sharding import PartitionSpec as P

STEPS_DEV = 4
GROUP = 16

diffusion = (0.2, 0.1)
interval_time = 0.03125
MESH = pl.DeviceIdType.MESH
single = np.float32


def cosine_basis(length):
    positions = np.arange(length, dtype=single)
    angles = single(np.pi) * (positions[:, None] + single(0.5)) * positions[None, :] / single(length)
    weight = np.where(positions == 0, np.sqrt(single(1.0 / length)), np.sqrt(single(2.0 / length)))
    return (np.cos(angles) * weight[None, :].astype(single)).astype(single)


def eigen_values(length):
    positions = np.arange(length, dtype=single)
    waves = np.sin(single(np.pi) * positions / single(2.0 * length))
    return (single(-4.0) * waves * waves).astype(single)


def halves(matrix):
    high = matrix.astype(ml_dtypes.bfloat16)
    low = (matrix - high.astype(np.float64)).astype(ml_dtypes.bfloat16)
    return high, low


def factors(rows, cols, time_step, rate, rank):
    basis_rows = cosine_basis(rows).astype(np.float64)
    basis_cols = cosine_basis(cols).astype(np.float64)
    spectrum = eigen_values(rows).astype(np.float64)[:, None] + eigen_values(cols).astype(np.float64)[None, :]
    factor = 1.0 / (1.0 - time_step * rate * spectrum)
    left, sizes, right = np.linalg.svd(factor)
    if rank is None:
        rank = 1
        while np.abs(factor - (left[:, :rank] * sizes[:rank]) @ right[:rank]).max() > 2.0**-26:
            rank += 1
        return rank
    left = left[:, :rank] * np.sqrt(sizes[:rank])
    right = right[:rank].T * np.sqrt(sizes[:rank])
    scale = left[0, 0]
    left[:, 0] /= scale
    right[:, 0] *= scale
    firsts = [basis_rows @ np.diag(left[:, k]) @ basis_rows.T for k in range(rank)]
    seconds = [basis_cols @ np.diag(right[:, k]) @ basis_cols.T for k in range(rank)]
    firsts[0] = firsts[0] - np.eye(rows)
    seconds[0] = seconds[0] - np.eye(cols)
    return firsts, seconds


@functools.lru_cache(maxsize=None)
def solve_tables(rows, cols, time_step):
    rank = max(factors(rows, cols, time_step, rate, None) for rate in diffusion)
    rank = max(rank, 2)
    species = [factors(rows, cols, time_step, rate, rank) for rate in diffusion]
    short = rank == 2
    blocks_high, blocks_low = [], []
    for k in range(rank):
        block = np.zeros((2 * cols, 2 * cols))
        block[:cols, :cols] = species[0][1][k]
        block[cols:, cols:] = species[1][1][k]
        high, low = halves(block)
        blocks_high.append(high)
        blocks_low.append(low)
    high = np.concatenate(blocks_high, 1)
    right_high = np.concatenate([high, high], 0)
    right_low = np.concatenate(blocks_low[: 1 if short else rank], 1)
    left_high, left_low = [], []
    for k in range(rank):
        high, low = halves(np.concatenate([species[0][0][k], species[1][0][k]], 0))
        left_high.append(high)
        left_low.append(low)
    if short:
        lefts = left_high + left_high[:1] + left_low[:1]
    else:
        lefts = left_high + left_high + left_low
    return right_high, right_low, np.concatenate(lefts, 1)


def kernel(devices, sizes, *refs):
    (initial_ref, guess_ref, feed_ref, kill_ref) = refs[:4]
    table_refs = (refs[4:7], refs[7:10], refs[10:13])
    traj_ref, resid_ref, coarse_ref, defect_ref = refs[13:17]
    (rates, b_buf, s_buf, r_buf, p_buf, e_buf, b_out, r_out, p_out) = refs[17:26]
    (send_b, recv_b, send_s, recv_s, send_r, recv_r, send_p, recv_p, send_e, recv_e) = refs[26:36]
    rows, cols = sizes
    groups = devices // GROUP
    me = lax.axis_index("tm")
    group = me // GROUP
    member = me % GROUP
    base = group * GROUP
    ahead = me + 2
    ahead_group = ahead // GROUP
    ahead_slot = ahead % GROUP
    ahead_valid = ahead < devices

    barrier = pltpu.get_barrier_semaphore()

    def greet(other):
        pl.semaphore_signal(barrier, inc=1, device_id=(other,), device_id_type=MESH)

    def greet_source(k, carry):
        source = base + k - 2

        @pl.when(jnp.logical_and(source >= 0, source != me))
        def _():
            greet(source)

        return carry

    lax.fori_loop(0, GROUP, greet_source, 0)

    @pl.when(me >= 1)
    def _():
        greet(me - 1)

    def greet_group(other, carry):
        greet(other * GROUP + member)
        return carry

    lax.fori_loop(0, group, greet_group, 0)

    left_half = lax.broadcasted_iota(jnp.int32, (rows, 2 * cols), 1) < cols
    fine_step = interval_time / STEPS_DEV
    steps = (fine_step, interval_time, interval_time * GROUP)
    feed = jnp.concatenate([feed_ref[...]] * 2, axis=1)
    kill = jnp.concatenate([kill_ref[...]] * 2, axis=1)
    source_term = jnp.where(left_half, feed, 0.0)
    decay = jnp.where(left_half, feed, feed + kill)
    for level, step in enumerate(steps):
        rates[2 * level] = 1.0 - step * decay
        rates[2 * level + 1] = step * source_term

    def pack(ref):
        return jnp.concatenate([ref[0], ref[1]], axis=1)

    def unpack(ref, index, value):
        ref[index, 0] = value[:, :cols]
        ref[index, 1] = value[:, cols:]

    def split(value):
        high = value.astype(jnp.bfloat16)
        low = (value - high.astype(jnp.float32)).astype(jnp.bfloat16)
        return high, low

    def dot(first, second):
        return jnp.dot(first, second, preferred_element_type=jnp.float32)

    def evolve(level, *states):
        step = steps[level]
        right_high, right_low, lefts = table_refs[level]
        terms = right_high.shape[1] // (2 * cols)
        signed = jnp.where(left_half, -step, step)
        reacted = []
        for state in states:
            swapped = pltpu.roll(state, cols, 1)
            second = jnp.where(left_half, swapped, state)
            uptake = state * swapped * second
            reacted.append(rates[2 * level] * state + rates[2 * level + 1] + signed * uptake)
        main = jnp.concatenate(reacted, 0) if len(reacted) > 1 else reacted[0]
        high, low = split(main)
        wide = dot(jnp.concatenate([high, low], 1), right_high[...])
        narrow = dot(high, right_low[...])
        parts = []
        for k in range(terms):
            part = wide[:, 2 * cols * k : 2 * cols * (k + 1)]
            if 2 * cols * k < right_low.shape[1]:
                part = part + narrow[:, 2 * cols * k : 2 * cols * (k + 1)]
            parts.append(part)
        first = main + parts[0]
        parts[0] = first
        columns = []
        for n in range(len(states)):
            pieces = [part[rows * n : rows * (n + 1)] for part in parts]
            if terms == 2:
                first_high, first_low = split(pieces[0])
                stack = [first_high, pieces[1].astype(jnp.bfloat16), first_low, first_high]
            else:
                pairs = [split(piece) for piece in pieces]
                stack = [a for a, b in pairs] + [b for a, b in pairs] + [a for a, b in pairs]
            columns.append(jnp.concatenate(stack, 0))
        stacked = jnp.concatenate(columns, 1) if len(columns) > 1 else columns[0]
        product = dot(lefts[...], stacked)
        finished = []
        for n in range(len(states)):
            piece = product[:, 2 * cols * n : 2 * cols * (n + 1)]
            small = jnp.where(left_half, piece[:rows], piece[rows:])
            finished.append(first[rows * n : rows * (n + 1)] + small)
        return finished

    start = pack(initial_ref)
    own = pack(guess_ref.at[0])

    def fine_turn(unused, pair):
        return tuple(evolve(0, *pair))

    relaxed, relaxed_zero = lax.fori_loop(0, STEPS_DEV, fine_turn, (own, start))
    r_out[...] = relaxed
    level_relaxed, level_relaxed_zero = evolve(1, relaxed, relaxed_zero)
    arrived, arrived_one = lax.fori_loop(0, STEPS_DEV, fine_turn, (relaxed, relaxed_zero))
    p_out[...] = arrived
    b_out[...] = arrived - level_relaxed

    targets = jnp.where(ahead_valid, GROUP - jnp.where(ahead_group == group, 1, 0), 0)
    targets = targets + jnp.where(me + 1 < devices, 1, 0) + groups - 1 - group

    @pl.when(targets > 0)
    def _():
        pl.semaphore_wait(barrier, targets)

    def remote(source, target, send, recv, other):
        return pltpu.make_async_remote_copy(
            src_ref=source, dst_ref=target, send_sem=send, recv_sem=recv,
            device_id=(other,), device_id_type=MESH,
        )

    def start_copy(i):
        return remote(s_src, s_buf, send_s.at[i], recv_s, ahead_group * GROUP + i)

    s_src = r_out

    def b_copy(i):
        return remote(b_out, b_buf.at[ahead_slot], send_b.at[i], recv_b.at[ahead_slot], ahead_group * GROUP + i)

    sends_start = jnp.logical_and(ahead_valid, ahead_slot == 0)

    def over_group(act):
        def turn(i, carry):
            @pl.when(jnp.logical_and(ahead_valid, ahead_group * GROUP + i != me))
            def _():
                act(i)

            return carry

        lax.fori_loop(0, GROUP, turn, 0)

    @pl.when(sends_start)
    def _():
        def turn(i, carry):
            start_copy(i).start()
            return carry

        lax.fori_loop(0, GROUP, turn, 0)

    over_group(lambda i: b_copy(i).start())
    r_copy = remote(r_out, r_buf, send_r, recv_r, me + 1)
    p_copy = remote(p_out, p_buf, send_p, recv_p, me + 2)

    @pl.when(me + 1 < devices)
    def _():
        r_copy.start()

    @pl.when(ahead_valid)
    def _():
        p_copy.start()

    @pl.when(jnp.logical_and(ahead_valid, ahead_group == group))
    def _():
        b_buf[ahead_slot] = b_out[...]

    @pl.when(group == 0)
    def _():
        (level_start,) = evolve(1, start)
        s_buf[...] = start
        b_buf[0] = relaxed_zero - level_start
        b_buf[1] = arrived_one - level_relaxed_zero

    @pl.when(me == 0)
    def _():
        r_buf[...] = relaxed_zero
        p_buf[...] = relaxed_zero

    @pl.when(me == 1)
    def _():
        p_buf[...] = arrived_one

    @pl.when(group > 0)
    def _():
        remote(r_out, s_buf, send_s.at[0], recv_s, me).wait_recv()

    group_start = s_buf[...]

    def level_turn(k, state):
        source = base + k - 2

        @pl.when(jnp.logical_and(source >= 0, source != me))
        def _():
            remote(b_out, b_buf.at[k], send_b.at[0], recv_b.at[k], me).wait_recv()

        (state,) = evolve(1, state)
        return state + b_buf[k]

    coarse_start, coarse_initial = evolve(2, group_start, start)
    closing = lax.fori_loop(0, GROUP, level_turn, group_start)
    e_buf[group] = closing - coarse_start

    def e_copy(other):
        return remote(e_buf.at[group], e_buf.at[group], send_e.at[other], recv_e.at[group], other * GROUP + member)

    def start_e(other, carry):
        e_copy(other).start()
        return carry

    lax.fori_loop(group + 1, groups, start_e, 0)

    def coarse_turn(other, pair):
        before, image = pair
        remote(e_buf.at[other], e_buf.at[other], send_e.at[0], recv_e.at[other], me).wait_recv()
        after = image + e_buf[other]
        (image,) = evolve(2, after)
        return after, image

    earlier, image = lax.fori_loop(0, group, coarse_turn, (start, coarse_initial))
    mine = image + e_buf[group]

    def replay(k, state):
        (state,) = evolve(1, state)
        return state + b_buf[k]

    prior = lax.fori_loop(0, member, replay, earlier)
    (ending,) = evolve(1, prior)
    ending = ending + b_buf[member]
    point = prior
    for i in range(STEPS_DEV - 1):
        (point,) = evolve(0, point)
        unpack(traj_ref, i, point)
    last = member == GROUP - 1
    unpack(traj_ref, STEPS_DEV - 1, jnp.where(last, mine, ending))
    unpack(coarse_ref, 0, mine)
    unpack(defect_ref, 0, jnp.where(last, ending - mine, 0.0))

    @pl.when(me >= 1)
    def _():
        remote(r_out, r_buf, send_r, recv_r, me).wait_recv()

    @pl.when(me >= 2)
    def _():
        remote(p_out, p_buf, send_p, recv_p, me).wait_recv()

    unpack(resid_ref, 0, p_buf[...] - r_buf[...])

    over_group(lambda i: b_copy(i).wait_send())

    @pl.when(sends_start)
    def _():
        def turn(i, carry):
            start_copy(i).wait_send()
            return carry

        lax.fori_loop(0, GROUP, turn, 0)

    @pl.when(me + 1 < devices)
    def _():
        r_copy.wait_send()

    @pl.when(ahead_valid)
    def _():
        p_copy.wait_send()

    def end_e(other, carry):
        e_copy(other).wait_send()
        return carry

    lax.fori_loop(group + 1, groups, end_e, 0)


def shards(devices, initial, coarse_guess, feed_rate, kill_rate):
    rows, cols = initial.shape[1:]
    groups = devices // GROUP
    steps = (interval_time / STEPS_DEV, interval_time, interval_time * GROUP)
    tables = []
    for step in steps:
        tables += [jnp.asarray(table) for table in solve_tables(rows, cols, step)]
    state = (rows, 2 * cols)
    block = (1,) + initial.shape
    dma = pltpu.SemaphoreType.DMA
    whole = pl.BlockSpec(memory_space=pltpu.VMEM)
    return pl.pallas_call(
        functools.partial(kernel, devices, (rows, cols)),
        out_shape=[
            jax.ShapeDtypeStruct((STEPS_DEV,) + initial.shape, jnp.float32),
            jax.ShapeDtypeStruct(block, jnp.float32),
            jax.ShapeDtypeStruct(block, jnp.float32),
            jax.ShapeDtypeStruct(block, jnp.float32),
        ],
        in_specs=[whole] * (4 + len(tables)),
        out_specs=[whole] * 4,
        scratch_shapes=[
            pltpu.VMEM((6,) + state, jnp.float32),
            pltpu.VMEM((GROUP,) + state, jnp.float32),
            pltpu.VMEM(state, jnp.float32),
            pltpu.VMEM(state, jnp.float32),
            pltpu.VMEM(state, jnp.float32),
            pltpu.VMEM((groups,) + state, jnp.float32),
            pltpu.VMEM(state, jnp.float32),
            pltpu.VMEM(state, jnp.float32),
            pltpu.VMEM(state, jnp.float32),
            dma((GROUP,)),
            dma((GROUP,)),
            dma((GROUP,)),
            dma,
            dma,
            dma,
            dma,
            dma,
            dma((groups,)),
            dma((groups,)),
        ],
        compiler_params=pltpu.CompilerParams(collective_id=0, has_side_effects=True),
    )(initial, coarse_guess, feed_rate, kill_rate, *tables)


def solution(mesh):
    spread = P("tm", None, None, None)
    return jax.shard_map(
        functools.partial(shards, mesh.shape["tm"]),
        mesh=mesh,
        in_specs=(P(), spread, P(), P()),
        out_specs=(spread, spread, spread, spread),
        check_vma=False,
    )
```

```python
import functools

import jax
import jax.numpy as jnp
import ml_dtypes
import numpy as np
from jax import lax
from jax.experimental import pallas as pl
from jax.experimental.pallas import tpu as pltpu
from jax.sharding import PartitionSpec as P

STEPS_DEV = 4
GROUP = 16

diffusion = (0.2, 0.1)
interval_time = 0.03125
MESH = pl.DeviceIdType.MESH
single = np.float32


def cosine_basis(length):
    positions = np.arange(length, dtype=single)
    angles = single(np.pi) * (positions[:, None] + single(0.5)) * positions[None, :] / single(length)
    weight = np.where(positions == 0, np.sqrt(single(1.0 / length)), np.sqrt(single(2.0 / length)))
    return (np.cos(angles) * weight[None, :].astype(single)).astype(single)


def eigen_values(length):
    positions = np.arange(length, dtype=single)
    waves = np.sin(single(np.pi) * positions / single(2.0 * length))
    return (single(-4.0) * waves * waves).astype(single)


def halves(matrix):
    high = matrix.astype(ml_dtypes.bfloat16)
    low = (matrix - high.astype(np.float64)).astype(ml_dtypes.bfloat16)
    return high, low


def factors(rows, cols, time_step, rate, rank):
    basis_rows = cosine_basis(rows).astype(np.float64)
    basis_cols = cosine_basis(cols).astype(np.float64)
    spectrum = eigen_values(rows).astype(np.float64)[:, None] + eigen_values(cols).astype(np.float64)[None, :]
    factor = 1.0 / (1.0 - time_step * rate * spectrum)
    left, sizes, right = np.linalg.svd(factor)
    if rank is None:
        rank = 1
        while np.abs(factor - (left[:, :rank] * sizes[:rank]) @ right[:rank]).max() > 2.0**-26:
            rank += 1
        return rank
    left = left[:, :rank] * np.sqrt(sizes[:rank])
    right = right[:rank].T * np.sqrt(sizes[:rank])
    scale = left[0, 0]
    left[:, 0] /= scale
    right[:, 0] *= scale
    firsts = [basis_rows @ np.diag(left[:, k]) @ basis_rows.T for k in range(rank)]
    seconds = [basis_cols @ np.diag(right[:, k]) @ basis_cols.T for k in range(rank)]
    firsts[0] = firsts[0] - np.eye(rows)
    seconds[0] = seconds[0] - np.eye(cols)
    return firsts, seconds


@functools.lru_cache(maxsize=None)
def solve_tables(rows, cols, time_step):
    rank = max(factors(rows, cols, time_step, rate, None) for rate in diffusion)
    rank = max(rank, 2)
    species = [factors(rows, cols, time_step, rate, rank) for rate in diffusion]
    short = rank == 2
    blocks_high, blocks_low = [], []
    for k in range(rank):
        block = np.zeros((2 * cols, 2 * cols))
        block[:cols, :cols] = species[0][1][k]
        block[cols:, cols:] = species[1][1][k]
        high, low = halves(block)
        blocks_high.append(high)
        blocks_low.append(low)
    high = np.concatenate(blocks_high, 1)
    right_high = np.concatenate([high, high], 0)
    right_low = np.concatenate(blocks_low[: 1 if short else rank], 1)
    left_high, left_low = [], []
    for k in range(rank):
        high, low = halves(np.concatenate([species[0][0][k], species[1][0][k]], 0))
        left_high.append(high)
        left_low.append(low)
    if short:
        lefts = left_high + left_high[:1] + left_low[:1]
    else:
        lefts = left_high + left_high + left_low
    return right_high, right_low, np.concatenate(lefts, 1)


def kernel(devices, sizes, *refs):
    (initial_ref, guess_ref, feed_ref, kill_ref) = refs[:4]
    table_refs = (refs[4:7], refs[7:10], refs[10:13])
    packed_ref = refs[13]
    (rates, b_buf, s_buf, r_buf, p_buf, e_buf, c_buf, b_out, r_out, s_out, p_out, c_out) = refs[14:26]
    (send_b, recv_b, send_s, recv_s, send_r, recv_r, send_p, recv_p, send_e, recv_e, send_c, recv_c) = refs[26:38]
    rows, cols = sizes
    groups = devices // GROUP
    me = lax.axis_index("tm")
    group = me // GROUP
    member = me % GROUP
    base = group * GROUP
    slot = (member + 2) % GROUP
    wraps = member >= GROUP - 2
    works = jnp.logical_or(group > 0, jnp.logical_not(wraps))
    passes_guess = jnp.logical_and(wraps, group < groups - 1)
    takes_guess = jnp.logical_and(wraps, group > 0)
    sends_start = jnp.logical_and(group > 0, member == GROUP - 2)
    sends_relaxed = jnp.logical_or(group > 0, member < GROUP - 1)

    barrier = pltpu.get_barrier_semaphore()

    def greet(other):
        pl.semaphore_signal(barrier, inc=1, device_id=(other,), device_id_type=MESH)

    def peer(i):
        return base + (member + 1 + i) % GROUP

    def greet_peer(i, carry):
        greet(peer(i))
        return carry

    def greet_group(other, carry):
        greet(other * GROUP + member)
        return carry

    lax.fori_loop(0, group, greet_group, 0)

    @pl.when(takes_guess)
    def _():
        greet(me - GROUP)

    lax.fori_loop(0, GROUP - 1, greet_peer, 0)

    def await_barrier():
        pl.semaphore_wait(barrier, GROUP - 1 + groups - 1 - group + jnp.where(passes_guess, 1, 0))

    def remote(source, target, send, recv, other):
        return pltpu.make_async_remote_copy(
            src_ref=source, dst_ref=target, send_sem=send, recv_sem=recv,
            device_id=(other,), device_id_type=MESH,
        )

    left_half = lax.broadcasted_iota(jnp.int32, (rows, 2 * cols), 1) < cols
    fine_step = interval_time / STEPS_DEV
    steps = (fine_step, interval_time, interval_time * GROUP)
    feed = jnp.concatenate([feed_ref[...]] * 2, axis=1)
    kill = jnp.concatenate([kill_ref[...]] * 2, axis=1)
    source_term = jnp.where(left_half, feed, 0.0)
    decay = jnp.where(left_half, feed, feed + kill)
    for level, step in enumerate(steps):
        rates[2 * level] = 1.0 - step * decay
        rates[2 * level + 1] = step * source_term

    def pack(ref):
        return jnp.concatenate([ref[0], ref[1]], axis=1)

    def split(value):
        high = value.astype(jnp.bfloat16)
        low = (value - high.astype(jnp.float32)).astype(jnp.bfloat16)
        return high, low

    def dot(first, second):
        return jnp.dot(first, second, preferred_element_type=jnp.float32)

    def evolve(level, *states):
        step = steps[level]
        right_high, right_low, lefts = table_refs[level]
        terms = right_high.shape[1] // (2 * cols)
        signed = jnp.where(left_half, -step, step)
        reacted = []
        for state in states:
            swapped = pltpu.roll(state, cols, 1)
            second = jnp.where(left_half, swapped, state)
            uptake = state * swapped * second
            reacted.append(rates[2 * level] * state + rates[2 * level + 1] + signed * uptake)
        main = jnp.concatenate(reacted, 0) if len(reacted) > 1 else reacted[0]
        high, low = split(main)
        wide = dot(jnp.concatenate([high, low], 1), right_high[...])
        narrow = dot(high, right_low[...])
        parts = []
        for k in range(terms):
            part = wide[:, 2 * cols * k : 2 * cols * (k + 1)]
            if 2 * cols * k < right_low.shape[1]:
                part = part + narrow[:, 2 * cols * k : 2 * cols * (k + 1)]
            parts.append(part)
        first = main + parts[0]
        parts[0] = first
        columns = []
        for n in range(len(states)):
            pieces = [part[rows * n : rows * (n + 1)] for part in parts]
            if terms == 2:
                first_high, first_low = split(pieces[0])
                stack = [first_high, pieces[1].astype(jnp.bfloat16), first_low, first_high]
            else:
                pairs = [split(piece) for piece in pieces]
                stack = [a for a, b in pairs] + [b for a, b in pairs] + [a for a, b in pairs]
            columns.append(jnp.concatenate(stack, 0))
        stacked = jnp.concatenate(columns, 1) if len(columns) > 1 else columns[0]
        product = dot(lefts[...], stacked)
        finished = []
        for n in range(len(states)):
            piece = product[:, 2 * cols * n : 2 * cols * (n + 1)]
            small = jnp.where(left_half, piece[:rows], piece[rows:])
            finished.append(first[rows * n : rows * (n + 1)] + small)
        return finished

    start = pack(initial_ref)
    own = pack(guess_ref.at[0])
    c_out[...] = own

    @pl.when(jnp.logical_not(takes_guess))
    def _():
        c_buf[...] = own

    guess_copy = remote(c_out, c_buf, send_c, recv_c, me + GROUP)

    @pl.when(wraps)
    def _():
        await_barrier()

    @pl.when(passes_guess)
    def _():
        guess_copy.start()

    @pl.when(takes_guess)
    def _():
        remote(c_out, c_buf, send_c, recv_c, me).wait_recv()

    def fine_turn(unused, pair):
        return tuple(evolve(0, *pair))

    side = jnp.where(sends_start, own, start)
    relaxed, relaxed_zero = lax.fori_loop(0, STEPS_DEV, fine_turn, (c_buf[...], side))
    r_out[...] = jnp.where(sends_start, relaxed_zero, relaxed)
    s_out[...] = relaxed

    def s_copy(i):
        return remote(s_out, s_buf, send_s.at[i], recv_s, peer(i))

    def b_copy(i):
        return remote(b_out, b_buf.at[slot], send_b.at[i], recv_b.at[slot], peer(i))

    def over_peers(act):
        def turn(i, carry):
            act(i)
            return carry

        lax.fori_loop(0, GROUP - 1, turn, 0)

    @pl.when(sends_start)
    def _():
        over_peers(lambda i: s_copy(i).start())

    arrived, arrived_one = lax.fori_loop(0, STEPS_DEV, fine_turn, (relaxed, relaxed_zero))
    level_relaxed, level_relaxed_zero = evolve(1, relaxed, relaxed_zero)
    p_out[...] = arrived
    b_out[...] = arrived - level_relaxed
    r_copy = remote(r_out, r_buf, send_r, recv_r, base + (member + 1) % GROUP)
    p_copy = remote(p_out, p_buf, send_p, recv_p, base + slot)

    @pl.when(jnp.logical_not(wraps))
    def _():
        await_barrier()

    @pl.when(works)
    def _():
        over_peers(lambda i: b_copy(i).start())
        p_copy.start()
        b_buf[slot] = b_out[...]

    @pl.when(sends_relaxed)
    def _():
        r_copy.start()

    @pl.when(group == 0)
    def _():
        (level_start,) = evolve(1, start)
        s_buf[...] = start
        b_buf[0] = relaxed_zero - level_start
        b_buf[1] = arrived_one - level_relaxed_zero

    @pl.when(me == 0)
    def _():
        r_buf[...] = relaxed_zero
        p_buf[...] = relaxed_zero

    @pl.when(me == 1)
    def _():
        p_buf[...] = arrived_one

    @pl.when(sends_start)
    def _():
        s_buf[...] = s_out[...]

    @pl.when(jnp.logical_and(group > 0, jnp.logical_not(sends_start)))
    def _():
        remote(s_out, s_buf, send_s.at[0], recv_s, me).wait_recv()

    group_start = s_buf[...]

    def level_turn(k, state):
        @pl.when(jnp.logical_and(base + k >= 2, k != slot))
        def _():
            remote(b_out, b_buf.at[k], send_b.at[0], recv_b.at[k], me).wait_recv()

        (state,) = evolve(1, state)
        return state + b_buf[k]

    coarse_start, coarse_initial = evolve(2, group_start, start)
    closing = lax.fori_loop(0, GROUP, level_turn, group_start)
    e_buf[group] = closing - coarse_start

    def e_copy(other):
        return remote(e_buf.at[group], e_buf.at[group], send_e.at[other], recv_e.at[group], other * GROUP + member)

    def start_e(other, carry):
        e_copy(other).start()
        return carry

    lax.fori_loop(group + 1, groups, start_e, 0)

    def coarse_turn(other, pair):
        before, image = pair
        remote(e_buf.at[other], e_buf.at[other], send_e.at[0], recv_e.at[other], me).wait_recv()
        after = image + e_buf[other]
        (image,) = evolve(2, after)
        return after, image

    earlier, image = lax.fori_loop(0, group, coarse_turn, (start, coarse_initial))
    mine = image + e_buf[group]

    def replay(k, state):
        (state,) = evolve(1, state)
        return state + b_buf[k]

    prior = lax.fori_loop(0, member, replay, earlier)
    (ending,) = evolve(1, prior)
    ending = ending + b_buf[member]
    point = prior
    for i in range(STEPS_DEV - 1):
        (point,) = evolve(0, point)
        packed_ref[i] = point
    last = member == GROUP - 1
    packed_ref[STEPS_DEV - 1] = jnp.where(last, mine, ending)
    packed_ref[STEPS_DEV + 1] = mine
    packed_ref[STEPS_DEV + 2] = jnp.where(last, ending - mine, 0.0)

    @pl.when(me >= 1)
    def _():
        remote(r_out, r_buf, send_r, recv_r, me).wait_recv()

    @pl.when(me >= 2)
    def _():
        remote(p_out, p_buf, send_p, recv_p, me).wait_recv()

    packed_ref[STEPS_DEV] = p_buf[...] - r_buf[...]

    @pl.when(works)
    def _():
        over_peers(lambda i: b_copy(i).wait_send())
        p_copy.wait_send()

    @pl.when(sends_start)
    def _():
        over_peers(lambda i: s_copy(i).wait_send())

    @pl.when(sends_relaxed)
    def _():
        r_copy.wait_send()

    @pl.when(passes_guess)
    def _():
        guess_copy.wait_send()

    def end_e(other, carry):
        e_copy(other).wait_send()
        return carry

    lax.fori_loop(group + 1, groups, end_e, 0)


def unpack(packed_ref, traj_ref, resid_ref, coarse_ref, defect_ref):
    cols = packed_ref.shape[2] // 2
    places = [(traj_ref, i) for i in range(STEPS_DEV)] + [(resid_ref, 0), (coarse_ref, 0), (defect_ref, 0)]
    for i, (ref, index) in enumerate(places):
        ref[index, 0] = packed_ref[i, :, :cols]
        ref[index, 1] = packed_ref[i, :, cols:]


def shards(devices, initial, coarse_guess, feed_rate, kill_rate):
    rows, cols = initial.shape[1:]
    groups = devices // GROUP
    steps = (interval_time / STEPS_DEV, interval_time, interval_time * GROUP)
    tables = []
    for step in steps:
        tables += [jnp.asarray(table) for table in solve_tables(rows, cols, step)]
    state = (rows, 2 * cols)
    block = (1,) + initial.shape
    dma = pltpu.SemaphoreType.DMA
    whole = pl.BlockSpec(memory_space=pltpu.VMEM)
    buffer = pltpu.VMEM(state, jnp.float32)
    packed = pl.pallas_call(
        functools.partial(kernel, devices, (rows, cols)),
        out_shape=jax.ShapeDtypeStruct((STEPS_DEV + 3,) + state, jnp.float32),
        in_specs=[whole] * (4 + len(tables)),
        out_specs=whole,
        scratch_shapes=[
            pltpu.VMEM((6,) + state, jnp.float32),
            pltpu.VMEM((GROUP,) + state, jnp.float32),
            buffer,
            buffer,
            buffer,
            pltpu.VMEM((groups,) + state, jnp.float32),
        ]
        + [buffer] * 6
        + [dma((GROUP,)), dma((GROUP,)), dma((GROUP,))]
        + [dma] * 5
        + [dma((groups,)), dma((groups,)), dma, dma],
        compiler_params=pltpu.CompilerParams(collective_id=0, has_side_effects=True),
    )(initial, coarse_guess, feed_rate, kill_rate, *tables)
    return pl.pallas_call(
        unpack,
        out_shape=[
            jax.ShapeDtypeStruct((STEPS_DEV,) + initial.shape, jnp.float32),
            jax.ShapeDtypeStruct(block, jnp.float32),
            jax.ShapeDtypeStruct(block, jnp.float32),
            jax.ShapeDtypeStruct(block, jnp.float32),
        ],
        in_specs=[whole],
        out_specs=[whole] * 4,
    )(packed)


def solution(mesh):
    spread = P("tm", None, None, None)
    return jax.shard_map(
        functools.partial(shards, mesh.shape["tm"]),
        mesh=mesh,
        in_specs=(P(), spread, P(), P()),
        out_specs=(spread, spread, spread, spread),
        check_vma=False,
    )
```

```python
import functools

import jax
import jax.numpy as jnp
import ml_dtypes
import numpy as np
from jax import lax
from jax.experimental import pallas as pl
from jax.experimental.pallas import tpu as pltpu
from jax.sharding import PartitionSpec as P

STEPS_DEV = 4
GROUP = 16

diffusion = (0.2, 0.1)
interval_time = 0.03125
MESH = pl.DeviceIdType.MESH
single = np.float32


def cosine_basis(length):
    positions = np.arange(length, dtype=single)
    angles = single(np.pi) * (positions[:, None] + single(0.5)) * positions[None, :] / single(length)
    weight = np.where(positions == 0, np.sqrt(single(1.0 / length)), np.sqrt(single(2.0 / length)))
    return (np.cos(angles) * weight[None, :].astype(single)).astype(single)


def eigen_values(length):
    positions = np.arange(length, dtype=single)
    waves = np.sin(single(np.pi) * positions / single(2.0 * length))
    return (single(-4.0) * waves * waves).astype(single)


def halves(matrix):
    high = matrix.astype(ml_dtypes.bfloat16)
    low = (matrix - high.astype(np.float64)).astype(ml_dtypes.bfloat16)
    return high, low


def factors(rows, cols, time_step, rate, rank):
    basis_rows = cosine_basis(rows).astype(np.float64)
    basis_cols = cosine_basis(cols).astype(np.float64)
    spectrum = eigen_values(rows).astype(np.float64)[:, None] + eigen_values(cols).astype(np.float64)[None, :]
    factor = 1.0 / (1.0 - time_step * rate * spectrum)
    left, sizes, right = np.linalg.svd(factor)
    if rank is None:
        rank = 1
        while np.abs(factor - (left[:, :rank] * sizes[:rank]) @ right[:rank]).max() > 2.0**-26:
            rank += 1
        return rank
    left = left[:, :rank] * np.sqrt(sizes[:rank])
    right = right[:rank].T * np.sqrt(sizes[:rank])
    scale = left[0, 0]
    left[:, 0] /= scale
    right[:, 0] *= scale
    firsts = [basis_rows @ np.diag(left[:, k]) @ basis_rows.T for k in range(rank)]
    seconds = [basis_cols @ np.diag(right[:, k]) @ basis_cols.T for k in range(rank)]
    firsts[0] = firsts[0] - np.eye(rows)
    seconds[0] = seconds[0] - np.eye(cols)
    return firsts, seconds


@functools.lru_cache(maxsize=None)
def solve_tables(rows, cols, time_step):
    rank = max(factors(rows, cols, time_step, rate, None) for rate in diffusion)
    rank = max(rank, 2)
    species = [factors(rows, cols, time_step, rate, rank) for rate in diffusion]
    short = rank == 2
    rights, lefts = [], []
    for firsts, seconds in species:
        highs, lows = [], []
        for second in seconds:
            high, low = halves(second)
            highs += [high] * 2
            lows += [low] * 2
        high = np.concatenate(highs, 1)
        low = np.concatenate(lows, 1)
        rights.append(np.concatenate([high, high, low, np.zeros_like(low)], 0))
        pairs = [halves(first) for first in firsts]
        highs = [high for high, low in pairs]
        lows = [low for high, low in pairs]
        if short:
            lefts.append(np.concatenate(highs + highs[:1] + lows[:1], 1))
        else:
            lefts.append(np.concatenate(highs + highs + lows, 1))
    return np.stack(rights), np.stack(lefts)


def kernel(devices, sizes, *refs):
    (initial_ref, guess_ref, feed_ref, kill_ref) = refs[:4]
    table_refs = (refs[4:6], refs[6:8], refs[8:10])
    packed_ref = refs[10]
    (rates, b_buf, s_buf, r_buf, p_buf, e_buf, c_buf, b_out, r_out, s_out, p_out, c_out) = refs[11:23]
    (send_b, recv_b, send_s, recv_s, send_r, recv_r, send_p, recv_p, send_e, recv_e, send_c, recv_c) = refs[23:35]
    rows, cols = sizes
    groups = devices // GROUP
    me = lax.axis_index("tm")
    group = me // GROUP
    member = me % GROUP
    base = group * GROUP
    slot = (member + 2) % GROUP
    wraps = member >= GROUP - 2
    works = jnp.logical_or(group > 0, jnp.logical_not(wraps))
    passes_guess = jnp.logical_and(wraps, group < groups - 1)
    takes_guess = jnp.logical_and(wraps, group > 0)
    sends_start = jnp.logical_and(group > 0, member == GROUP - 2)
    sends_relaxed = jnp.logical_or(group > 0, member < GROUP - 1)

    barrier = pltpu.get_barrier_semaphore()

    def greet(other):
        pl.semaphore_signal(barrier, inc=1, device_id=(other,), device_id_type=MESH)

    def peer(i):
        return base + (member + 1 + i) % GROUP

    def greet_peer(i, carry):
        greet(peer(i))
        return carry

    def greet_group(other, carry):
        greet(other * GROUP + member)
        return carry

    lax.fori_loop(0, group, greet_group, 0)

    @pl.when(takes_guess)
    def _():
        greet(me - GROUP)

    lax.fori_loop(0, GROUP - 1, greet_peer, 0)

    def await_barrier():
        pl.semaphore_wait(barrier, GROUP - 1 + groups - 1 - group + jnp.where(passes_guess, 1, 0))

    def remote(source, target, send, recv, other):
        return pltpu.make_async_remote_copy(
            src_ref=source, dst_ref=target, send_sem=send, recv_sem=recv,
            device_id=(other,), device_id_type=MESH,
        )

    left_half = lax.broadcasted_iota(jnp.int32, (rows, 2 * cols), 1) < cols
    fine_step = interval_time / STEPS_DEV
    steps = (fine_step, interval_time, interval_time * GROUP)
    feed = jnp.concatenate([feed_ref[...]] * 2, axis=1)
    kill = jnp.concatenate([kill_ref[...]] * 2, axis=1)
    for level, step in enumerate(steps):
        rates[3 * level] = 1.0 - step * feed
        rates[3 * level + 1] = step * feed
        rates[3 * level + 2] = 1.0 - step * (feed + kill)

    def double(value):
        return jnp.concatenate([value, value], axis=1)

    def join(state):
        return jnp.where(left_half, state[0], state[1])

    def spread(value):
        turned = pltpu.roll(value, cols, 1)
        return jnp.where(left_half, value, turned), jnp.where(left_half, turned, value)

    def plus(state, other):
        return state[0] + other[0], state[1] + other[1]

    def minus(state, other):
        return state[0] - other[0], state[1] - other[1]

    def split(value):
        high = value.astype(jnp.bfloat16)
        low = (value - high.astype(jnp.float32)).astype(jnp.bfloat16)
        return high, low

    def dot(first, second):
        return jnp.dot(first, second, preferred_element_type=jnp.float32)

    def solve(level, kind, values):
        rights, lefts = table_refs[level]
        terms = rights.shape[2] // (2 * cols)
        main = jnp.concatenate(values, 0) if len(values) > 1 else values[0]
        mask = jnp.concatenate([left_half] * len(values), 0) if len(values) > 1 else left_half
        high = main.astype(jnp.bfloat16)
        wide = high.astype(jnp.float32)
        mixed = jnp.where(mask, wide, main - wide).astype(jnp.bfloat16)
        product = dot(jnp.concatenate([mixed, high], 1), rights[kind])
        parts = [product[:, 2 * cols * k : 2 * cols * (k + 1)] for k in range(terms)]
        first = main + parts[0]
        parts[0] = first
        columns = []
        for n in range(len(values)):
            pieces = [part[rows * n : rows * (n + 1)] for part in parts]
            if terms == 2:
                first_high, first_low = split(pieces[0])
                stack = [first_high, pieces[1].astype(jnp.bfloat16), first_low, first_high]
            else:
                pairs = [split(piece) for piece in pieces]
                stack = [a for a, b in pairs] + [b for a, b in pairs] + [a for a, b in pairs]
            columns.append(jnp.concatenate(stack, 0))
        stacked = jnp.concatenate(columns, 1) if len(columns) > 1 else columns[0]
        small = dot(lefts[kind], stacked)
        return [
            first[rows * n : rows * (n + 1)] + small[:, 2 * cols * n : 2 * cols * (n + 1)]
            for n in range(len(values))
        ]

    def evolve(level, *states):
        step = steps[level]
        reacted = ([], [])
        for substrate, catalyst in states:
            uptake = step * (substrate * (catalyst * catalyst))
            reacted[0].append(rates[3 * level] * substrate + rates[3 * level + 1] - uptake)
            reacted[1].append(rates[3 * level + 2] * catalyst + uptake)
        return list(zip(solve(level, 0, reacted[0]), solve(level, 1, reacted[1])))

    start = double(initial_ref[0]), double(initial_ref[1])
    own = double(guess_ref[0, 0]), double(guess_ref[0, 1])
    own_packed = join(own)
    c_out[...] = own_packed

    @pl.when(jnp.logical_not(takes_guess))
    def _():
        c_buf[...] = own_packed

    guess_copy = remote(c_out, c_buf, send_c, recv_c, me + GROUP)

    @pl.when(wraps)
    def _():
        await_barrier()

    @pl.when(passes_guess)
    def _():
        guess_copy.start()

    @pl.when(takes_guess)
    def _():
        remote(c_out, c_buf, send_c, recv_c, me).wait_recv()

    def fine_turn(unused, pair):
        return tuple(evolve(0, *pair))

    side = tuple(jnp.where(sends_start, mine, theirs) for mine, theirs in zip(own, start))
    relaxed, relaxed_zero = lax.fori_loop(0, STEPS_DEV, fine_turn, (spread(c_buf[...]), side))
    relaxed_packed = join(relaxed)
    zero_packed = join(relaxed_zero)
    r_out[...] = jnp.where(sends_start, zero_packed, relaxed_packed)
    s_out[...] = relaxed_packed

    def s_copy(i):
        return remote(s_out, s_buf, send_s.at[i], recv_s, peer(i))

    def b_copy(i):
        return remote(b_out, b_buf.at[slot], send_b.at[i], recv_b.at[slot], peer(i))

    def over_peers(act):
        def turn(i, carry):
            act(i)
            return carry

        lax.fori_loop(0, GROUP - 1, turn, 0)

    @pl.when(sends_start)
    def _():
        over_peers(lambda i: s_copy(i).start())

    arrived, arrived_one = lax.fori_loop(0, STEPS_DEV, fine_turn, (relaxed, relaxed_zero))
    level_relaxed, level_relaxed_zero = evolve(1, relaxed, relaxed_zero)
    p_out[...] = join(arrived)
    b_out[...] = join(minus(arrived, level_relaxed))
    r_copy = remote(r_out, r_buf, send_r, recv_r, base + (member + 1) % GROUP)
    p_copy = remote(p_out, p_buf, send_p, recv_p, base + slot)

    @pl.when(jnp.logical_not(wraps))
    def _():
        await_barrier()

    @pl.when(works)
    def _():
        over_peers(lambda i: b_copy(i).start())
        p_copy.start()
        b_buf[slot] = b_out[...]

    @pl.when(sends_relaxed)
    def _():
        r_copy.start()

    @pl.when(group == 0)
    def _():
        (level_start,) = evolve(1, start)
        s_buf[...] = join(start)
        b_buf[0] = join(minus(relaxed_zero, level_start))
        b_buf[1] = join(minus(arrived_one, level_relaxed_zero))

    @pl.when(me == 0)
    def _():
        r_buf[...] = zero_packed
        p_buf[...] = zero_packed

    @pl.when(me == 1)
    def _():
        p_buf[...] = join(arrived_one)

    @pl.when(sends_start)
    def _():
        s_buf[...] = s_out[...]

    @pl.when(jnp.logical_and(group > 0, jnp.logical_not(sends_start)))
    def _():
        remote(s_out, s_buf, send_s.at[0], recv_s, me).wait_recv()

    group_start = spread(s_buf[...])

    def level_turn(k, state):
        @pl.when(jnp.logical_and(base + k >= 2, k != slot))
        def _():
            remote(b_out, b_buf.at[k], send_b.at[0], recv_b.at[k], me).wait_recv()

        (state,) = evolve(1, state)
        return plus(state, spread(b_buf[k]))

    coarse_start, coarse_initial = evolve(2, group_start, start)
    opens = group == 0
    opening = tuple(jnp.where(opens, a, b) for a, b in zip(relaxed_zero, group_start))
    closing = lax.fori_loop(jnp.where(opens, 1, 0), GROUP, level_turn, opening)
    e_buf[group] = join(minus(closing, coarse_start))

    def e_copy(other):
        return remote(e_buf.at[group], e_buf.at[group], send_e.at[other], recv_e.at[group], other * GROUP + member)

    def start_e(other, carry):
        e_copy(other).start()
        return carry

    lax.fori_loop(group + 1, groups, start_e, 0)

    def await_e(other):
        remote(e_buf.at[other], e_buf.at[other], send_e.at[0], recv_e.at[other], me).wait_recv()

    def coarse_turn(other, before):
        await_e(other)
        (image,) = evolve(2, before)
        return plus(image, spread(e_buf[other]))

    @pl.when(group > 0)
    def _():
        await_e(0)

    first_coarse = plus(coarse_initial, spread(e_buf[0]))
    earlier = tuple(jnp.where(opens, a, b) for a, b in zip(start, first_coarse))
    earlier = lax.fori_loop(1, group, coarse_turn, earlier)

    def replay(k, state):
        (state,) = evolve(1, state)
        return plus(state, spread(b_buf[k]))

    prior = lax.fori_loop(0, member, replay, earlier)
    (mine,) = evolve(2, earlier)
    mine = join(mine) + e_buf[group]
    (ending,) = evolve(1, prior)
    ending = join(ending) + b_buf[member]
    point = prior
    for i in range(STEPS_DEV - 1):
        (point,) = evolve(0, point)
        packed_ref[i] = join(point)
    last = member == GROUP - 1
    packed_ref[STEPS_DEV - 1] = jnp.where(last, mine, ending)
    packed_ref[STEPS_DEV + 1] = mine
    packed_ref[STEPS_DEV + 2] = jnp.where(last, ending - mine, 0.0)

    @pl.when(me >= 1)
    def _():
        remote(r_out, r_buf, send_r, recv_r, me).wait_recv()

    @pl.when(me >= 2)
    def _():
        remote(p_out, p_buf, send_p, recv_p, me).wait_recv()

    packed_ref[STEPS_DEV] = p_buf[...] - r_buf[...]

    @pl.when(works)
    def _():
        over_peers(lambda i: b_copy(i).wait_send())
        p_copy.wait_send()

    @pl.when(sends_start)
    def _():
        over_peers(lambda i: s_copy(i).wait_send())

    @pl.when(sends_relaxed)
    def _():
        r_copy.wait_send()

    @pl.when(passes_guess)
    def _():
        guess_copy.wait_send()

    def end_e(other, carry):
        e_copy(other).wait_send()
        return carry

    lax.fori_loop(group + 1, groups, end_e, 0)


def unpack(packed_ref, traj_ref, resid_ref, coarse_ref, defect_ref):
    cols = packed_ref.shape[2] // 2
    places = [(traj_ref, i) for i in range(STEPS_DEV)] + [(resid_ref, 0), (coarse_ref, 0), (defect_ref, 0)]
    for i, (ref, index) in enumerate(places):
        ref[index, 0] = packed_ref[i, :, :cols]
        ref[index, 1] = packed_ref[i, :, cols:]


def shards(devices, initial, coarse_guess, feed_rate, kill_rate):
    rows, cols = initial.shape[1:]
    groups = devices // GROUP
    steps = (interval_time / STEPS_DEV, interval_time, interval_time * GROUP)
    tables = []
    for step in steps:
        tables += [jnp.asarray(table) for table in solve_tables(rows, cols, step)]
    state = (rows, 2 * cols)
    block = (1,) + initial.shape
    dma = pltpu.SemaphoreType.DMA
    whole = pl.BlockSpec(memory_space=pltpu.VMEM)
    buffer = pltpu.VMEM(state, jnp.float32)
    packed = pl.pallas_call(
        functools.partial(kernel, devices, (rows, cols)),
        out_shape=jax.ShapeDtypeStruct((STEPS_DEV + 3,) + state, jnp.float32),
        in_specs=[whole] * (4 + len(tables)),
        out_specs=whole,
        scratch_shapes=[
            pltpu.VMEM((9,) + state, jnp.float32),
            pltpu.VMEM((GROUP,) + state, jnp.float32),
            buffer,
            buffer,
            buffer,
            pltpu.VMEM((groups,) + state, jnp.float32),
        ]
        + [buffer] * 6
        + [dma((GROUP,)), dma((GROUP,)), dma((GROUP,))]
        + [dma] * 5
        + [dma((groups,)), dma((groups,)), dma, dma],
        compiler_params=pltpu.CompilerParams(collective_id=0, has_side_effects=True),
    )(initial, coarse_guess, feed_rate, kill_rate, *tables)
    return pl.pallas_call(
        unpack,
        out_shape=[
            jax.ShapeDtypeStruct((STEPS_DEV,) + initial.shape, jnp.float32),
            jax.ShapeDtypeStruct(block, jnp.float32),
            jax.ShapeDtypeStruct(block, jnp.float32),
            jax.ShapeDtypeStruct(block, jnp.float32),
        ],
        in_specs=[whole],
        out_specs=[whole] * 4,
    )(packed)


def solution(mesh):
    spread = P("tm", None, None, None)
    return jax.shard_map(
        functools.partial(shards, mesh.shape["tm"]),
        mesh=mesh,
        in_specs=(P(), spread, P(), P()),
        out_specs=(spread, spread, spread, spread),
        check_vma=False,
    )
```

```python
import functools

import jax
import jax.numpy as jnp
import ml_dtypes
import numpy as np
from jax import lax
from jax.experimental import pallas as pl
from jax.experimental.pallas import tpu as pltpu
from jax.sharding import PartitionSpec as P

STEPS_DEV = 4
GROUP = 16

diffusion = (0.2, 0.1)
interval_time = 0.03125
MESH = pl.DeviceIdType.MESH
single = np.float32


def cosine_basis(length):
    positions = np.arange(length, dtype=single)
    angles = single(np.pi) * (positions[:, None] + single(0.5)) * positions[None, :] / single(length)
    weight = np.where(positions == 0, np.sqrt(single(1.0 / length)), np.sqrt(single(2.0 / length)))
    return (np.cos(angles) * weight[None, :].astype(single)).astype(single)


def eigen_values(length):
    positions = np.arange(length, dtype=single)
    waves = np.sin(single(np.pi) * positions / single(2.0 * length))
    return (single(-4.0) * waves * waves).astype(single)


def halves(matrix):
    high = matrix.astype(ml_dtypes.bfloat16)
    low = (matrix - high.astype(np.float64)).astype(ml_dtypes.bfloat16)
    return high, low


def factors(rows, cols, time_step, rate, rank):
    basis_rows = cosine_basis(rows).astype(np.float64)
    basis_cols = cosine_basis(cols).astype(np.float64)
    spectrum = eigen_values(rows).astype(np.float64)[:, None] + eigen_values(cols).astype(np.float64)[None, :]
    factor = 1.0 / (1.0 - time_step * rate * spectrum)
    left, sizes, right = np.linalg.svd(factor)
    if rank is None:
        rank = 1
        while np.abs(factor - (left[:, :rank] * sizes[:rank]) @ right[:rank]).max() > 2.0**-26:
            rank += 1
        return rank
    left = left[:, :rank] * np.sqrt(sizes[:rank])
    right = right[:rank].T * np.sqrt(sizes[:rank])
    scale = left[0, 0]
    left[:, 0] /= scale
    right[:, 0] *= scale
    firsts = [basis_rows @ np.diag(left[:, k]) @ basis_rows.T for k in range(rank)]
    seconds = [basis_cols @ np.diag(right[:, k]) @ basis_cols.T for k in range(rank)]
    firsts[0] = firsts[0] - np.eye(rows)
    seconds[0] = seconds[0] - np.eye(cols)
    return firsts, seconds


@functools.lru_cache(maxsize=None)
def solve_tables(rows, cols, time_step):
    rank = max(factors(rows, cols, time_step, rate, None) for rate in diffusion)
    rank = max(rank, 2)
    species = [factors(rows, cols, time_step, rate, rank) for rate in diffusion]
    short = rank == 2
    rights, lefts = [], []
    for firsts, seconds in species:
        highs, lows = [], []
        for second in seconds:
            high, low = halves(second)
            highs += [high] * 2
            lows += [low] * 2
        high = np.concatenate(highs, 1)
        low = np.concatenate(lows, 1)
        rights.append(np.concatenate([high, high, low, np.zeros_like(low)], 0))
        pairs = [halves(first) for first in firsts]
        highs = [high for high, low in pairs]
        lows = [low for high, low in pairs]
        if short:
            lefts.append(np.concatenate(highs + highs[:1] + lows[:1], 1))
        else:
            lefts.append(np.concatenate(highs + highs + lows, 1))
    return np.stack(rights), np.stack(lefts)


def kernel(devices, sizes, *refs):
    (initial_ref, guess_ref, feed_ref, kill_ref) = refs[:4]
    table_refs = (refs[4:6], refs[6:8], refs[8:10])
    packed_ref = refs[10]
    (rates, b_buf, s_buf, r_buf, p_buf, e_buf, c_buf, b_out, r_out, s_out, p_out, c_out) = refs[11:23]
    (send_b, recv_b, send_s, recv_s, send_r, recv_r, send_p, recv_p, send_e, recv_e, send_c, recv_c) = refs[23:35]
    rows, cols = sizes
    groups = devices // GROUP
    me = lax.axis_index("tm")
    group = me // GROUP
    member = me % GROUP
    base = group * GROUP
    slot = (member + 2) % GROUP
    wraps = member >= GROUP - 2
    works = jnp.logical_or(group > 0, jnp.logical_not(wraps))
    passes_guess = jnp.logical_and(wraps, group < groups - 1)
    takes_guess = jnp.logical_and(wraps, group > 0)
    sends_start = jnp.logical_and(group > 0, member == GROUP - 2)
    sends_relaxed = jnp.logical_or(group > 0, member < GROUP - 1)

    barrier = pltpu.get_barrier_semaphore()

    def greet(other):
        pl.semaphore_signal(barrier, inc=1, device_id=(other,), device_id_type=MESH)

    def peer(i):
        return base + (member + 1 + i) % GROUP

    def greet_peer(i, carry):
        greet(peer(i))
        return carry

    def greet_group(other, carry):
        greet(other * GROUP + member)
        return carry

    lax.fori_loop(0, group, greet_group, 0)

    @pl.when(takes_guess)
    def _():
        greet(me - GROUP)

    lax.fori_loop(0, GROUP - 1, greet_peer, 0)

    def await_barrier():
        pl.semaphore_wait(barrier, GROUP - 1 + groups - 1 - group + jnp.where(passes_guess, 1, 0))

    def remote(source, target, send, recv, other):
        return pltpu.make_async_remote_copy(
            src_ref=source, dst_ref=target, send_sem=send, recv_sem=recv,
            device_id=(other,), device_id_type=MESH,
        )

    left_half = lax.broadcasted_iota(jnp.int32, (rows, 2 * cols), 1) < cols
    fine_step = interval_time / STEPS_DEV
    steps = (fine_step, interval_time, interval_time * GROUP)
    feed = jnp.concatenate([feed_ref[...]] * 2, axis=1)
    kill = jnp.concatenate([kill_ref[...]] * 2, axis=1)
    for level, step in enumerate(steps):
        rates[3 * level] = 1.0 - step * feed
        rates[3 * level + 1] = step * feed
        rates[3 * level + 2] = 1.0 - step * (feed + kill)

    def double(value):
        return jnp.concatenate([value, value], axis=1)

    def join(state):
        return jnp.where(left_half, state[0], state[1])

    def spread(value):
        turned = pltpu.roll(value, cols, 1)
        return jnp.where(left_half, value, turned), jnp.where(left_half, turned, value)

    def plus(state, other):
        return state[0] + other[0], state[1] + other[1]

    def minus(state, other):
        return state[0] - other[0], state[1] - other[1]

    def split(value):
        high = value.astype(jnp.bfloat16)
        low = (value - high.astype(jnp.float32)).astype(jnp.bfloat16)
        return high, low

    def dot(first, second):
        return jnp.dot(first, second, preferred_element_type=jnp.float32)

    def stacked_rows(values):
        return jnp.concatenate(values, 0) if len(values) > 1 else values[0]

    def spectral(level, kind, main):
        count = main.shape[0] // rows
        high = main.astype(jnp.bfloat16)
        wide = high.astype(jnp.float32)
        mixed = jnp.where(stacked_rows([left_half] * count), wide, main - wide).astype(jnp.bfloat16)
        return dot(jnp.concatenate([mixed, high], 1), table_refs[level][0][kind])

    def gather_terms(main, product):
        count = main.shape[0] // rows
        terms = product.shape[1] // (2 * cols)
        parts = [product[:, 2 * cols * k : 2 * cols * (k + 1)] for k in range(terms)]
        first = main + parts[0]
        parts[0] = first
        columns = []
        for n in range(count):
            pieces = [part[rows * n : rows * (n + 1)] for part in parts]
            if terms == 2:
                first_high, first_low = split(pieces[0])
                stack = [first_high, pieces[1].astype(jnp.bfloat16), first_low, first_high]
            else:
                pairs = [split(piece) for piece in pieces]
                stack = [a for a, b in pairs] + [b for a, b in pairs] + [a for a, b in pairs]
            columns.append(jnp.concatenate(stack, 0))
        return first, jnp.concatenate(columns, 1) if count > 1 else columns[0]

    def solve(level, mains):
        products = [spectral(level, kind, main) for kind, main in enumerate(mains)]
        gathered = [gather_terms(main, product) for main, product in zip(mains, products)]
        smalls = [dot(table_refs[level][1][kind], stack) for kind, (first, stack) in enumerate(gathered)]
        count = mains[0].shape[0] // rows
        return [
            [first[rows * n : rows * (n + 1)] + small[:, 2 * cols * n : 2 * cols * (n + 1)] for n in range(count)]
            for (first, stack), small in zip(gathered, smalls)
        ]

    def evolve(level, *states):
        step = steps[level]
        reacted = ([], [])
        for substrate, catalyst in states:
            uptake = step * (substrate * (catalyst * catalyst))
            reacted[0].append(rates[3 * level] * substrate + rates[3 * level + 1] - uptake)
            reacted[1].append(rates[3 * level + 2] * catalyst + uptake)
        return list(zip(*solve(level, [stacked_rows(values) for values in reacted])))

    start = double(initial_ref[0]), double(initial_ref[1])
    own = double(guess_ref[0, 0]), double(guess_ref[0, 1])
    own_packed = join(own)
    c_out[...] = own_packed

    @pl.when(jnp.logical_not(takes_guess))
    def _():
        c_buf[...] = own_packed

    guess_copy = remote(c_out, c_buf, send_c, recv_c, me + GROUP)

    @pl.when(wraps)
    def _():
        await_barrier()

    @pl.when(passes_guess)
    def _():
        guess_copy.start()

    @pl.when(takes_guess)
    def _():
        remote(c_out, c_buf, send_c, recv_c, me).wait_recv()

    def fine_turn(unused, pair):
        return tuple(evolve(0, *pair))

    side = tuple(jnp.where(sends_start, mine, theirs) for mine, theirs in zip(own, start))
    relaxed, relaxed_zero = lax.fori_loop(0, STEPS_DEV, fine_turn, (spread(c_buf[...]), side))
    relaxed_packed = join(relaxed)
    zero_packed = join(relaxed_zero)
    r_out[...] = jnp.where(sends_start, zero_packed, relaxed_packed)
    s_out[...] = relaxed_packed

    def s_copy(i):
        return remote(s_out, s_buf, send_s.at[i], recv_s, peer(i))

    def b_copy(i):
        return remote(b_out, b_buf.at[slot], send_b.at[i], recv_b.at[slot], peer(i))

    def over_peers(act):
        def turn(i, carry):
            act(i)
            return carry

        lax.fori_loop(0, GROUP - 1, turn, 0)

    @pl.when(sends_start)
    def _():
        over_peers(lambda i: s_copy(i).start())

    arrived, arrived_one = lax.fori_loop(0, STEPS_DEV, fine_turn, (relaxed, relaxed_zero))
    level_relaxed, level_relaxed_zero = evolve(1, relaxed, relaxed_zero)
    p_out[...] = join(arrived)
    b_out[...] = join(minus(arrived, level_relaxed))
    r_copy = remote(r_out, r_buf, send_r, recv_r, base + (member + 1) % GROUP)
    p_copy = remote(p_out, p_buf, send_p, recv_p, base + slot)

    @pl.when(jnp.logical_not(wraps))
    def _():
        await_barrier()

    @pl.when(works)
    def _():
        over_peers(lambda i: b_copy(i).start())
        p_copy.start()
        b_buf[slot] = b_out[...]

    @pl.when(sends_relaxed)
    def _():
        r_copy.start()

    @pl.when(group == 0)
    def _():
        (level_start,) = evolve(1, start)
        s_buf[...] = join(start)
        b_buf[0] = join(minus(relaxed_zero, level_start))
        b_buf[1] = join(minus(arrived_one, level_relaxed_zero))

    @pl.when(me == 0)
    def _():
        r_buf[...] = zero_packed
        p_buf[...] = zero_packed

    @pl.when(me == 1)
    def _():
        p_buf[...] = join(arrived_one)

    @pl.when(sends_start)
    def _():
        s_buf[...] = s_out[...]

    @pl.when(jnp.logical_and(group > 0, jnp.logical_not(sends_start)))
    def _():
        remote(s_out, s_buf, send_s.at[0], recv_s, me).wait_recv()

    group_start = spread(s_buf[...])

    def level_turn(k, state):
        @pl.when(jnp.logical_and(base + k >= 2, k != slot))
        def _():
            remote(b_out, b_buf.at[k], send_b.at[0], recv_b.at[k], me).wait_recv()

        (state,) = evolve(1, state)
        return plus(state, spread(b_buf[k]))

    coarse_start, coarse_initial = evolve(2, group_start, start)
    opens = group == 0
    opening = tuple(jnp.where(opens, a, b) for a, b in zip(relaxed_zero, group_start))
    closing = lax.fori_loop(jnp.where(opens, 1, 0), GROUP, level_turn, opening)
    e_buf[group] = join(minus(closing, coarse_start))

    def e_copy(other):
        return remote(e_buf.at[group], e_buf.at[group], send_e.at[other], recv_e.at[group], other * GROUP + member)

    def start_e(other, carry):
        e_copy(other).start()
        return carry

    lax.fori_loop(group + 1, groups, start_e, 0)

    def await_e(other):
        remote(e_buf.at[other], e_buf.at[other], send_e.at[0], recv_e.at[other], me).wait_recv()

    def coarse_turn(other, before):
        await_e(other)
        (image,) = evolve(2, before)
        return plus(image, spread(e_buf[other]))

    @pl.when(group > 0)
    def _():
        await_e(0)

    first_coarse = plus(coarse_initial, spread(e_buf[0]))
    earlier = tuple(jnp.where(opens, a, b) for a, b in zip(start, first_coarse))
    earlier = lax.fori_loop(1, group, coarse_turn, earlier)

    def replay(k, state):
        (state,) = evolve(1, state)
        return plus(state, spread(b_buf[k]))

    prior = lax.fori_loop(0, member, replay, earlier)
    (mine,) = evolve(2, earlier)
    mine = join(mine) + e_buf[group]
    (ending,) = evolve(1, prior)
    ending = join(ending) + b_buf[member]
    point = prior
    for i in range(STEPS_DEV - 1):
        (point,) = evolve(0, point)
        packed_ref[i] = join(point)
    last = member == GROUP - 1
    packed_ref[STEPS_DEV - 1] = jnp.where(last, mine, ending)
    packed_ref[STEPS_DEV + 1] = mine
    packed_ref[STEPS_DEV + 2] = jnp.where(last, ending - mine, 0.0)

    @pl.when(me >= 1)
    def _():
        remote(r_out, r_buf, send_r, recv_r, me).wait_recv()

    @pl.when(me >= 2)
    def _():
        remote(p_out, p_buf, send_p, recv_p, me).wait_recv()

    packed_ref[STEPS_DEV] = p_buf[...] - r_buf[...]

    @pl.when(works)
    def _():
        over_peers(lambda i: b_copy(i).wait_send())
        p_copy.wait_send()

    @pl.when(sends_start)
    def _():
        over_peers(lambda i: s_copy(i).wait_send())

    @pl.when(sends_relaxed)
    def _():
        r_copy.wait_send()

    @pl.when(passes_guess)
    def _():
        guess_copy.wait_send()

    def end_e(other, carry):
        e_copy(other).wait_send()
        return carry

    lax.fori_loop(group + 1, groups, end_e, 0)


def unpack(packed_ref, traj_ref, resid_ref, coarse_ref, defect_ref):
    cols = packed_ref.shape[2] // 2
    places = [(traj_ref, i) for i in range(STEPS_DEV)] + [(resid_ref, 0), (coarse_ref, 0), (defect_ref, 0)]
    for i, (ref, index) in enumerate(places):
        ref[index, 0] = packed_ref[i, :, :cols]
        ref[index, 1] = packed_ref[i, :, cols:]


def shards(devices, initial, coarse_guess, feed_rate, kill_rate):
    rows, cols = initial.shape[1:]
    groups = devices // GROUP
    steps = (interval_time / STEPS_DEV, interval_time, interval_time * GROUP)
    tables = []
    for step in steps:
        tables += [jnp.asarray(table) for table in solve_tables(rows, cols, step)]
    state = (rows, 2 * cols)
    block = (1,) + initial.shape
    dma = pltpu.SemaphoreType.DMA
    whole = pl.BlockSpec(memory_space=pltpu.VMEM)
    buffer = pltpu.VMEM(state, jnp.float32)
    packed = pl.pallas_call(
        functools.partial(kernel, devices, (rows, cols)),
        out_shape=jax.ShapeDtypeStruct((STEPS_DEV + 3,) + state, jnp.float32),
        in_specs=[whole] * (4 + len(tables)),
        out_specs=whole,
        scratch_shapes=[
            pltpu.VMEM((9,) + state, jnp.float32),
            pltpu.VMEM((GROUP,) + state, jnp.float32),
            buffer,
            buffer,
            buffer,
            pltpu.VMEM((groups,) + state, jnp.float32),
        ]
        + [buffer] * 6
        + [dma((GROUP,)), dma((GROUP,)), dma((GROUP,))]
        + [dma] * 5
        + [dma((groups,)), dma((groups,)), dma, dma],
        compiler_params=pltpu.CompilerParams(collective_id=0, has_side_effects=True),
    )(initial, coarse_guess, feed_rate, kill_rate, *tables)
    return pl.pallas_call(
        unpack,
        out_shape=[
            jax.ShapeDtypeStruct((STEPS_DEV,) + initial.shape, jnp.float32),
            jax.ShapeDtypeStruct(block, jnp.float32),
            jax.ShapeDtypeStruct(block, jnp.float32),
            jax.ShapeDtypeStruct(block, jnp.float32),
        ],
        in_specs=[whole],
        out_specs=[whole] * 4,
    )(packed)


def solution(mesh):
    spread = P("tm", None, None, None)
    return jax.shard_map(
        functools.partial(shards, mesh.shape["tm"]),
        mesh=mesh,
        in_specs=(P(), spread, P(), P()),
        out_specs=(spread, spread, spread, spread),
        check_vma=False,
    )
```

```python
import functools

import jax
import jax.numpy as jnp
import ml_dtypes
import numpy as np
from jax import lax
from jax.experimental import pallas as pl
from jax.experimental.pallas import tpu as pltpu
from jax.sharding import PartitionSpec as P

STEPS_DEV = 4
GROUP = 16

diffusion = (0.2, 0.1)
interval_time = 0.03125
MESH = pl.DeviceIdType.MESH
single = np.float32


def cosine_basis(length):
    positions = np.arange(length, dtype=single)
    angles = single(np.pi) * (positions[:, None] + single(0.5)) * positions[None, :] / single(length)
    weight = np.where(positions == 0, np.sqrt(single(1.0 / length)), np.sqrt(single(2.0 / length)))
    return (np.cos(angles) * weight[None, :].astype(single)).astype(single)


def eigen_values(length):
    positions = np.arange(length, dtype=single)
    waves = np.sin(single(np.pi) * positions / single(2.0 * length))
    return (single(-4.0) * waves * waves).astype(single)


def halves(matrix):
    high = matrix.astype(ml_dtypes.bfloat16)
    low = (matrix - high.astype(np.float64)).astype(ml_dtypes.bfloat16)
    return high, low


def factors(rows, cols, time_step, rate, rank):
    basis_rows = cosine_basis(rows).astype(np.float64)
    basis_cols = cosine_basis(cols).astype(np.float64)
    spectrum = eigen_values(rows).astype(np.float64)[:, None] + eigen_values(cols).astype(np.float64)[None, :]
    factor = 1.0 / (1.0 - time_step * rate * spectrum)
    left, sizes, right = np.linalg.svd(factor)
    if rank is None:
        rank = 1
        while np.abs(factor - (left[:, :rank] * sizes[:rank]) @ right[:rank]).max() > 2.0**-26:
            rank += 1
        return rank
    left = left[:, :rank] * np.sqrt(sizes[:rank])
    right = right[:rank].T * np.sqrt(sizes[:rank])
    scale = left[0, 0]
    left[:, 0] /= scale
    right[:, 0] *= scale
    firsts = [basis_rows @ np.diag(left[:, k]) @ basis_rows.T for k in range(rank)]
    seconds = [basis_cols @ np.diag(right[:, k]) @ basis_cols.T for k in range(rank)]
    firsts[0] = firsts[0] - np.eye(rows)
    seconds[0] = seconds[0] - np.eye(cols)
    return firsts, seconds


@functools.lru_cache(maxsize=None)
def solve_tables(rows, cols, time_step):
    rank = max(factors(rows, cols, time_step, rate, None) for rate in diffusion)
    rank = max(rank, 2)
    species = [factors(rows, cols, time_step, rate, rank) for rate in diffusion]
    short = rank == 2
    rights, lefts = [], []
    for firsts, seconds in species:
        highs, lows = [], []
        for second in seconds:
            high, low = halves(second)
            highs += [high] * 2
            lows += [low] * 2
        high = np.concatenate(highs, 1)
        low = np.concatenate(lows, 1)
        rights.append(np.concatenate([high, high, low], 0))
        pairs = [halves(first) for first in firsts]
        highs = [high for high, low in pairs]
        lows = [low for high, low in pairs]
        if short:
            lefts.append(np.concatenate(highs + highs[:1] + lows[:1], 1))
        else:
            lefts.append(np.concatenate(highs + highs + lows, 1))
    return np.stack(rights), np.stack(lefts)


def kernel(devices, sizes, *refs):
    (initial_ref, guess_ref, feed_ref, kill_ref) = refs[:4]
    table_refs = (refs[4:6], refs[6:8], refs[8:10])
    packed_ref = refs[10]
    (rates, b_buf, s_buf, r_buf, p_buf, e_buf, b_out, r_out, p_out) = refs[11:20]
    (send_b, recv_b, send_s, recv_s, send_r, recv_r, send_p, recv_p, send_e, recv_e, send_f, send_o) = refs[20:32]
    rows, cols = sizes
    groups = devices // GROUP
    me = lax.axis_index("tm")
    group = me // GROUP
    member = me % GROUP
    base = group * GROUP
    slot = (member + 2) % GROUP
    wraps = member >= GROUP - 2
    forwards = jnp.logical_and(wraps, group < groups - 1)
    relays = jnp.logical_and(wraps, group > 0)
    first_wrap = member == GROUP - 2

    barrier = pltpu.get_barrier_semaphore()

    def greet(other):
        pl.semaphore_signal(barrier, inc=1, device_id=(other,), device_id_type=MESH)

    def peer(i):
        return base + (member + 1 + i) % GROUP

    def greet_peer(i, carry):
        greet(peer(i))
        return carry

    def greet_group(other, carry):
        greet(other * GROUP + member)
        return carry

    lax.fori_loop(0, group, greet_group, 0)

    @pl.when(jnp.logical_and(group > 0, member <= 1))
    def _():
        greet(me - 2)

    @pl.when(jnp.logical_and(group > 0, member == 0))
    def _():
        greet(me - 1)

    lax.fori_loop(0, GROUP - 1, greet_peer, 0)

    def await_barrier():
        pl.semaphore_wait(barrier, GROUP - 1 + groups - 1 - group + jnp.where(forwards, member - (GROUP - 3), 0))

    def remote(source, target, send, recv, other):
        return pltpu.make_async_remote_copy(
            src_ref=source, dst_ref=target, send_sem=send, recv_sem=recv,
            device_id=(other,), device_id_type=MESH,
        )

    left_half = lax.broadcasted_iota(jnp.int32, (rows, 2 * cols), 1) < cols
    fine_step = interval_time / STEPS_DEV
    steps = (fine_step, interval_time, interval_time * GROUP)
    feed = jnp.concatenate([feed_ref[...]] * 2, axis=1)
    kill = jnp.concatenate([kill_ref[...]] * 2, axis=1)
    for level, step in enumerate(steps):
        rates[3 * level] = 1.0 - step * feed
        rates[3 * level + 1] = step * feed
        rates[3 * level + 2] = 1.0 - step * (feed + kill)

    def double(value):
        return jnp.concatenate([value, value], axis=1)

    def join(state):
        return jnp.where(left_half, state[0], state[1])

    def spread(value):
        turned = pltpu.roll(value, cols, 1)
        return jnp.where(left_half, value, turned), jnp.where(left_half, turned, value)

    def plus(state, other):
        return state[0] + other[0], state[1] + other[1]

    def minus(state, other):
        return state[0] - other[0], state[1] - other[1]

    def split(value):
        high = value.astype(jnp.bfloat16)
        low = (value - high.astype(jnp.float32)).astype(jnp.bfloat16)
        return high, low

    def dot(first, second):
        return jnp.dot(first, second, preferred_element_type=jnp.float32)

    def stacked_rows(values):
        return jnp.concatenate(values, 0) if len(values) > 1 else values[0]

    def spectral(level, kind, main):
        count = main.shape[0] // rows
        high = main.astype(jnp.bfloat16)
        wide = high.astype(jnp.float32)
        mixed = jnp.where(stacked_rows([left_half] * count), wide, main - wide).astype(jnp.bfloat16)
        return dot(jnp.concatenate([mixed, high[:, :cols]], 1), table_refs[level][0][kind])

    def gather_terms(main, product):
        count = main.shape[0] // rows
        terms = product.shape[1] // (2 * cols)
        parts = [product[:, 2 * cols * k : 2 * cols * (k + 1)] for k in range(terms)]
        first = main + parts[0]
        parts[0] = first
        columns = []
        for n in range(count):
            pieces = [part[rows * n : rows * (n + 1)] for part in parts]
            if terms == 2:
                first_high, first_low = split(pieces[0])
                stack = [first_high, pieces[1].astype(jnp.bfloat16), first_low, first_high]
            else:
                pairs = [split(piece) for piece in pieces]
                stack = [a for a, b in pairs] + [b for a, b in pairs] + [a for a, b in pairs]
            columns.append(jnp.concatenate(stack, 0))
        return first, jnp.concatenate(columns, 1) if count > 1 else columns[0]

    def solve(level, mains):
        products = [spectral(level, kind, main) for kind, main in enumerate(mains)]
        gathered = [gather_terms(main, product) for main, product in zip(mains, products)]
        smalls = [dot(table_refs[level][1][kind], stack) for kind, (first, stack) in enumerate(gathered)]
        count = mains[0].shape[0] // rows
        return [
            [first[rows * n : rows * (n + 1)] + small[:, 2 * cols * n : 2 * cols * (n + 1)] for n in range(count)]
            for (first, stack), small in zip(gathered, smalls)
        ]

    def evolve(level, *states):
        step = steps[level]
        reacted = ([], [])
        for substrate, catalyst in states:
            uptake = step * (substrate * (catalyst * catalyst))
            reacted[0].append(rates[3 * level] * substrate + rates[3 * level + 1] - uptake)
            reacted[1].append(rates[3 * level + 2] * catalyst + uptake)
        return list(zip(*solve(level, [stacked_rows(values) for values in reacted])))

    start = double(initial_ref[0]), double(initial_ref[1])
    own = double(guess_ref[0, 0]), double(guess_ref[0, 1])

    def fine_turn(unused, pair):
        return tuple(evolve(0, *pair))

    relaxed, relaxed_zero = lax.fori_loop(0, STEPS_DEV, fine_turn, (own, start))
    zero_packed = join(relaxed_zero)
    r_out[...] = join(relaxed)

    def over_peers(act):
        def turn(i, carry):
            act(i)
            return carry

        lax.fori_loop(0, GROUP - 1, turn, 0)

    arrived, arrived_one = lax.fori_loop(0, STEPS_DEV, fine_turn, (relaxed, relaxed_zero))
    level_relaxed, level_relaxed_zero = evolve(1, relaxed, relaxed_zero)
    p_out[...] = join(arrived)
    b_out[...] = join(minus(arrived, level_relaxed))
    r_copy = remote(r_out, r_buf, send_r, recv_r, me + 1)
    p_copy = remote(p_out, p_buf, send_p, recv_p, me + 2)
    s_forward = remote(r_out, s_buf, send_o, recv_s, me + GROUP)
    b_forward = remote(b_out, b_buf.at[slot], send_f, recv_b.at[slot], me + GROUP)

    def b_copy(i):
        return remote(b_out, b_buf.at[slot], send_b.at[i], recv_b.at[slot], peer(i))

    def b_relay(i):
        return remote(b_buf.at[slot], b_buf.at[slot], send_b.at[i], recv_b.at[slot], peer(i))

    def s_relay(i):
        return remote(s_buf, s_buf, send_s.at[i], recv_s, peer(i))

    await_barrier()

    @pl.when(jnp.logical_and(forwards, first_wrap))
    def _():
        s_forward.start()

    @pl.when(forwards)
    def _():
        b_forward.start()

    @pl.when(jnp.logical_not(wraps))
    def _():
        over_peers(lambda i: b_copy(i).start())
        b_buf[slot] = b_out[...]

    @pl.when(me + 2 < devices)
    def _():
        p_copy.start()

    @pl.when(me + 1 < devices)
    def _():
        r_copy.start()

    @pl.when(group == 0)
    def _():
        (level_start,) = evolve(1, start)
        s_buf[...] = join(start)
        b_buf[0] = join(minus(relaxed_zero, level_start))
        b_buf[1] = join(minus(arrived_one, level_relaxed_zero))

    @pl.when(me == 0)
    def _():
        r_buf[...] = zero_packed
        p_buf[...] = zero_packed

    @pl.when(me == 1)
    def _():
        p_buf[...] = join(arrived_one)

    @pl.when(group > 0)
    def _():
        remote(r_out, s_buf, send_o, recv_s, me).wait_recv()

    @pl.when(jnp.logical_and(relays, first_wrap))
    def _():
        over_peers(lambda i: s_relay(i).start())

    @pl.when(relays)
    def _():
        b_forward.wait_recv()
        over_peers(lambda i: b_relay(i).start())

    group_start = spread(s_buf[...])

    def level_turn(k, state):
        @pl.when(jnp.logical_and(base + k >= 2, k != slot))
        def _():
            remote(b_out, b_buf.at[k], send_b.at[0], recv_b.at[k], me).wait_recv()

        (state,) = evolve(1, state)
        return plus(state, spread(b_buf[k]))

    coarse_start, coarse_initial = evolve(2, group_start, start)
    opens = group == 0
    opening = tuple(jnp.where(opens, a, b) for a, b in zip(relaxed_zero, group_start))
    closing = lax.fori_loop(jnp.where(opens, 1, 0), GROUP, level_turn, opening)
    e_buf[group] = join(minus(closing, coarse_start))

    def e_copy(other):
        return remote(e_buf.at[group], e_buf.at[group], send_e.at[other], recv_e.at[group], other * GROUP + member)

    def start_e(other, carry):
        e_copy(other).start()
        return carry

    lax.fori_loop(group + 1, groups, start_e, 0)

    def await_e(other):
        remote(e_buf.at[other], e_buf.at[other], send_e.at[0], recv_e.at[other], me).wait_recv()

    def coarse_turn(other, before):
        await_e(other)
        (image,) = evolve(2, before)
        return plus(image, spread(e_buf[other]))

    @pl.when(group > 0)
    def _():
        await_e(0)

    first_coarse = plus(coarse_initial, spread(e_buf[0]))
    earlier = tuple(jnp.where(opens, a, b) for a, b in zip(start, first_coarse))
    earlier = lax.fori_loop(1, group, coarse_turn, earlier)

    def replay(k, state):
        (state,) = evolve(1, state)
        return plus(state, spread(b_buf[k]))

    prior = lax.fori_loop(0, member, replay, earlier)
    (mine,) = evolve(2, earlier)
    mine = join(mine) + e_buf[group]
    (ending,) = evolve(1, prior)
    ending = join(ending) + b_buf[member]
    point = prior
    for i in range(STEPS_DEV - 1):
        (point,) = evolve(0, point)
        packed_ref[i] = join(point)
    last = member == GROUP - 1
    packed_ref[STEPS_DEV - 1] = jnp.where(last, mine, ending)
    packed_ref[STEPS_DEV + 1] = mine
    packed_ref[STEPS_DEV + 2] = jnp.where(last, ending - mine, 0.0)

    @pl.when(me >= 1)
    def _():
        remote(r_out, r_buf, send_r, recv_r, me).wait_recv()

    @pl.when(me >= 2)
    def _():
        remote(p_out, p_buf, send_p, recv_p, me).wait_recv()

    packed_ref[STEPS_DEV] = p_buf[...] - r_buf[...]

    @pl.when(jnp.logical_not(wraps))
    def _():
        over_peers(lambda i: b_copy(i).wait_send())

    @pl.when(relays)
    def _():
        over_peers(lambda i: b_relay(i).wait_send())

    @pl.when(jnp.logical_and(relays, first_wrap))
    def _():
        over_peers(lambda i: s_relay(i).wait_send())

    @pl.when(jnp.logical_and(forwards, first_wrap))
    def _():
        s_forward.wait_send()

    @pl.when(forwards)
    def _():
        b_forward.wait_send()

    @pl.when(me + 2 < devices)
    def _():
        p_copy.wait_send()

    @pl.when(me + 1 < devices)
    def _():
        r_copy.wait_send()

    def end_e(other, carry):
        e_copy(other).wait_send()
        return carry

    lax.fori_loop(group + 1, groups, end_e, 0)


def unpack(packed_ref, traj_ref, resid_ref, coarse_ref, defect_ref):
    cols = packed_ref.shape[2] // 2
    places = [(traj_ref, i) for i in range(STEPS_DEV)] + [(resid_ref, 0), (coarse_ref, 0), (defect_ref, 0)]
    for i, (ref, index) in enumerate(places):
        ref[index, 0] = packed_ref[i, :, :cols]
        ref[index, 1] = packed_ref[i, :, cols:]


def shards(devices, initial, coarse_guess, feed_rate, kill_rate):
    rows, cols = initial.shape[1:]
    groups = devices // GROUP
    steps = (interval_time / STEPS_DEV, interval_time, interval_time * GROUP)
    tables = []
    for step in steps:
        tables += [jnp.asarray(table) for table in solve_tables(rows, cols, step)]
    state = (rows, 2 * cols)
    block = (1,) + initial.shape
    dma = pltpu.SemaphoreType.DMA
    whole = pl.BlockSpec(memory_space=pltpu.VMEM)
    buffer = pltpu.VMEM(state, jnp.float32)
    packed = pl.pallas_call(
        functools.partial(kernel, devices, (rows, cols)),
        out_shape=jax.ShapeDtypeStruct((STEPS_DEV + 3,) + state, jnp.float32),
        in_specs=[whole] * (4 + len(tables)),
        out_specs=whole,
        scratch_shapes=[
            pltpu.VMEM((9,) + state, jnp.float32),
            pltpu.VMEM((GROUP,) + state, jnp.float32),
            buffer,
            buffer,
            buffer,
            pltpu.VMEM((groups,) + state, jnp.float32),
        ]
        + [buffer] * 3
        + [dma((GROUP,)), dma((GROUP,)), dma((GROUP,))]
        + [dma] * 5
        + [dma((groups,)), dma((groups,)), dma, dma],
        compiler_params=pltpu.CompilerParams(collective_id=0, has_side_effects=True),
    )(initial, coarse_guess, feed_rate, kill_rate, *tables)
    return pl.pallas_call(
        unpack,
        out_shape=[
            jax.ShapeDtypeStruct((STEPS_DEV,) + initial.shape, jnp.float32),
            jax.ShapeDtypeStruct(block, jnp.float32),
            jax.ShapeDtypeStruct(block, jnp.float32),
            jax.ShapeDtypeStruct(block, jnp.float32),
        ],
        in_specs=[whole],
        out_specs=[whole] * 4,
    )(packed)


def solution(mesh):
    spread = P("tm", None, None, None)
    return jax.shard_map(
        functools.partial(shards, mesh.shape["tm"]),
        mesh=mesh,
        in_specs=(P(), spread, P(), P()),
        out_specs=(spread, spread, spread, spread),
        check_vma=False,
    )
```

```python
import functools

import jax
import jax.numpy as jnp
import ml_dtypes
import numpy as np
from jax import lax
from jax.experimental import pallas as pl
from jax.experimental.pallas import tpu as pltpu
from jax.sharding import PartitionSpec as P

STEPS_DEV = 4
GROUP = 16
CHUNK = 5

diffusion = (0.2, 0.1)
interval_time = 0.03125
MESH = pl.DeviceIdType.MESH
single = np.float32


def cosine_basis(length):
    positions = np.arange(length, dtype=single)
    angles = single(np.pi) * (positions[:, None] + single(0.5)) * positions[None, :] / single(length)
    weight = np.where(positions == 0, np.sqrt(single(1.0 / length)), np.sqrt(single(2.0 / length)))
    return (np.cos(angles) * weight[None, :].astype(single)).astype(single)


def eigen_values(length):
    positions = np.arange(length, dtype=single)
    waves = np.sin(single(np.pi) * positions / single(2.0 * length))
    return (single(-4.0) * waves * waves).astype(single)


def halves(matrix):
    high = matrix.astype(ml_dtypes.bfloat16)
    low = (matrix - high.astype(np.float64)).astype(ml_dtypes.bfloat16)
    return high, low


def factors(rows, cols, time_step, rate, rank):
    basis_rows = cosine_basis(rows).astype(np.float64)
    basis_cols = cosine_basis(cols).astype(np.float64)
    spectrum = eigen_values(rows).astype(np.float64)[:, None] + eigen_values(cols).astype(np.float64)[None, :]
    factor = 1.0 / (1.0 - time_step * rate * spectrum)
    left, sizes, right = np.linalg.svd(factor)
    if rank is None:
        rank = 1
        while np.abs(factor - (left[:, :rank] * sizes[:rank]) @ right[:rank]).max() > 2.0**-26:
            rank += 1
        return rank
    left = left[:, :rank] * np.sqrt(sizes[:rank])
    right = right[:rank].T * np.sqrt(sizes[:rank])
    scale = left[0, 0]
    left[:, 0] /= scale
    right[:, 0] *= scale
    firsts = [basis_rows @ np.diag(left[:, k]) @ basis_rows.T for k in range(rank)]
    seconds = [basis_cols @ np.diag(right[:, k]) @ basis_cols.T for k in range(rank)]
    firsts[0] = firsts[0] - np.eye(rows)
    seconds[0] = seconds[0] - np.eye(cols)
    return firsts, seconds


@functools.lru_cache(maxsize=None)
def solve_tables(rows, cols, time_step):
    rank = max(factors(rows, cols, time_step, rate, None) for rate in diffusion)
    rank = max(rank, 2)
    species = [factors(rows, cols, time_step, rate, rank) for rate in diffusion]
    short = rank == 2
    rights, lefts = [], []
    for firsts, seconds in species:
        highs, lows = [], []
        for second in seconds:
            high, low = halves(second)
            highs += [high] * 2
            lows += [low] * 2
        high = np.concatenate(highs, 1)
        low = np.concatenate(lows, 1)
        rights.append(np.concatenate([high, high, low], 0))
        pairs = [halves(first) for first in firsts]
        highs = [high for high, low in pairs]
        lows = [low for high, low in pairs]
        if short:
            lefts.append(np.concatenate(highs + highs[:1] + lows[:1], 1))
        else:
            lefts.append(np.concatenate(highs + highs + lows, 1))
    return np.stack(rights), np.stack(lefts)


def kernel(devices, sizes, *refs):
    (initial_ref, guess_ref, feed_ref, kill_ref) = refs[:4]
    table_refs = (refs[4:6], refs[6:8], refs[8:10])
    packed_ref = refs[10]
    (rates, b_buf, s_buf, r_buf, p_buf, e_buf, b_out, r_out, p_out) = refs[11:20]
    (send_b, recv_b, send_s, recv_s, send_r, recv_r, send_p, recv_p, send_e, recv_e, send_f, send_o) = refs[20:32]
    rows, cols = sizes
    groups = devices // GROUP
    me = lax.axis_index("tm")
    group = me // GROUP
    member = me % GROUP
    base = group * GROUP
    slot = (member + 2) % GROUP
    wraps = member >= GROUP - 2
    forwards = jnp.logical_and(wraps, group < groups - 1)
    relays = jnp.logical_and(wraps, group > 0)
    first_wrap = member == GROUP - 2

    barrier = pltpu.get_barrier_semaphore()

    def greet(other):
        pl.semaphore_signal(barrier, inc=1, device_id=(other,), device_id_type=MESH)

    def peer(i):
        return base + (member + 1 + i) % GROUP

    def greet_peer(i, carry):
        greet(peer(i))
        return carry

    def greet_group(other, carry):
        greet(other * GROUP + member)
        return carry

    lax.fori_loop(0, group, greet_group, 0)

    @pl.when(jnp.logical_and(group > 0, member <= 1))
    def _():
        greet(me - 2)

    @pl.when(jnp.logical_and(group > 0, member == 0))
    def _():
        greet(me - 1)

    lax.fori_loop(0, GROUP - 1, greet_peer, 0)

    def await_barrier():
        pl.semaphore_wait(barrier, GROUP - 1 + groups - 1 - group + jnp.where(forwards, member - (GROUP - 3), 0))

    def remote(source, target, send, recv, other):
        return pltpu.make_async_remote_copy(
            src_ref=source, dst_ref=target, send_sem=send, recv_sem=recv,
            device_id=(other,), device_id_type=MESH,
        )

    left_half = lax.broadcasted_iota(jnp.int32, (rows, 2 * cols), 1) < cols
    fine_step = interval_time / STEPS_DEV
    steps = (fine_step, interval_time, interval_time * GROUP)
    feed = jnp.concatenate([feed_ref[...]] * 2, axis=1)
    kill = jnp.concatenate([kill_ref[...]] * 2, axis=1)
    for level, step in enumerate(steps):
        rates[3 * level] = 1.0 - step * feed
        rates[3 * level + 1] = step * feed
        rates[3 * level + 2] = 1.0 - step * (feed + kill)

    def double(value):
        return jnp.concatenate([value, value], axis=1)

    def join(state):
        return jnp.where(left_half, state[0], state[1])

    def spread(value):
        turned = pltpu.roll(value, cols, 1)
        return jnp.where(left_half, value, turned), jnp.where(left_half, turned, value)

    def plus(state, other):
        return state[0] + other[0], state[1] + other[1]

    def minus(state, other):
        return state[0] - other[0], state[1] - other[1]

    def split(value):
        high = value.astype(jnp.bfloat16)
        low = (value - high.astype(jnp.float32)).astype(jnp.bfloat16)
        return high, low

    def dot(first, second):
        return jnp.dot(first, second, preferred_element_type=jnp.float32)

    def stacked_rows(values):
        return jnp.concatenate(values, 0) if len(values) > 1 else values[0]

    def spectral(level, kind, main):
        count = main.shape[0] // rows
        high = main.astype(jnp.bfloat16)
        wide = high.astype(jnp.float32)
        mixed = jnp.where(stacked_rows([left_half] * count), wide, main - wide).astype(jnp.bfloat16)
        return dot(jnp.concatenate([mixed, high[:, :cols]], 1), table_refs[level][0][kind])

    def gather_terms(main, product):
        count = main.shape[0] // rows
        terms = product.shape[1] // (2 * cols)
        parts = [product[:, 2 * cols * k : 2 * cols * (k + 1)] for k in range(terms)]
        first = main + parts[0]
        parts[0] = first
        columns = []
        for n in range(count):
            pieces = [part[rows * n : rows * (n + 1)] for part in parts]
            if terms == 2:
                first_high, first_low = split(pieces[0])
                stack = [first_high, pieces[1].astype(jnp.bfloat16), first_low, first_high]
            else:
                pairs = [split(piece) for piece in pieces]
                stack = [a for a, b in pairs] + [b for a, b in pairs] + [a for a, b in pairs]
            columns.append(jnp.concatenate(stack, 0))
        return first, jnp.concatenate(columns, 1) if count > 1 else columns[0]

    def solve(level, mains):
        products = [spectral(level, kind, main) for kind, main in enumerate(mains)]
        gathered = [gather_terms(main, product) for main, product in zip(mains, products)]
        smalls = [dot(table_refs[level][1][kind], stack) for kind, (first, stack) in enumerate(gathered)]
        count = mains[0].shape[0] // rows
        return [
            [first[rows * n : rows * (n + 1)] + small[:, 2 * cols * n : 2 * cols * (n + 1)] for n in range(count)]
            for (first, stack), small in zip(gathered, smalls)
        ]

    def evolve(level, *states):
        step = steps[level]
        reacted = ([], [])
        for substrate, catalyst in states:
            uptake = step * (substrate * (catalyst * catalyst))
            reacted[0].append(rates[3 * level] * substrate + rates[3 * level + 1] - uptake)
            reacted[1].append(rates[3 * level + 2] * catalyst + uptake)
        return list(zip(*solve(level, [stacked_rows(values) for values in reacted])))

    start = double(initial_ref[0]), double(initial_ref[1])
    own = double(guess_ref[0, 0]), double(guess_ref[0, 1])

    def fine_turn(unused, pair):
        return tuple(evolve(0, *pair))

    relaxed, relaxed_zero = lax.fori_loop(0, STEPS_DEV, fine_turn, (own, start), unroll=True)
    zero_packed = join(relaxed_zero)
    r_out[...] = join(relaxed)

    def over_peers(act):
        def turn(i, carry):
            act(i)
            return carry

        lax.fori_loop(0, GROUP - 1, turn, 0)

    arrived, arrived_one = lax.fori_loop(0, STEPS_DEV, fine_turn, (relaxed, relaxed_zero), unroll=True)
    level_relaxed, level_relaxed_zero = evolve(1, relaxed, relaxed_zero)
    p_out[...] = join(arrived)
    b_out[...] = join(minus(arrived, level_relaxed))
    r_copy = remote(r_out, r_buf, send_r, recv_r, me + 1)
    p_copy = remote(p_out, p_buf, send_p, recv_p, me + 2)
    s_forward = remote(r_out, s_buf, send_o, recv_s, me + GROUP)
    b_forward = remote(b_out, b_buf.at[slot], send_f, recv_b.at[slot], me + GROUP)

    def b_copy(i):
        return remote(b_out, b_buf.at[slot], send_b.at[i], recv_b.at[slot], peer(i))

    def b_relay(i):
        return remote(b_buf.at[slot], b_buf.at[slot], send_b.at[i], recv_b.at[slot], peer(i))

    def s_relay(i):
        return remote(s_buf, s_buf, send_s.at[i], recv_s, peer(i))

    await_barrier()

    @pl.when(jnp.logical_and(forwards, first_wrap))
    def _():
        s_forward.start()

    @pl.when(forwards)
    def _():
        b_forward.start()

    @pl.when(jnp.logical_not(wraps))
    def _():
        over_peers(lambda i: b_copy(i).start())
        b_buf[slot] = b_out[...]

    @pl.when(me + 2 < devices)
    def _():
        p_copy.start()

    @pl.when(me + 1 < devices)
    def _():
        r_copy.start()

    @pl.when(group == 0)
    def _():
        (level_start,) = evolve(1, start)
        s_buf[...] = join(start)
        b_buf[0] = join(minus(relaxed_zero, level_start))
        b_buf[1] = join(minus(arrived_one, level_relaxed_zero))

    @pl.when(me == 0)
    def _():
        r_buf[...] = zero_packed
        p_buf[...] = zero_packed

    @pl.when(me == 1)
    def _():
        p_buf[...] = join(arrived_one)

    @pl.when(group > 0)
    def _():
        remote(r_out, s_buf, send_o, recv_s, me).wait_recv()

    @pl.when(jnp.logical_and(relays, first_wrap))
    def _():
        over_peers(lambda i: s_relay(i).start())

    @pl.when(relays)
    def _():
        b_forward.wait_recv()
        over_peers(lambda i: b_relay(i).start())

    group_start = spread(s_buf[...])

    def await_b(k):
        @pl.when(jnp.logical_and(base + k >= 2, k != slot))
        def _():
            remote(b_out, b_buf.at[k], send_b.at[0], recv_b.at[k], me).wait_recv()

    def level_turn(k, state):
        (state,) = evolve(1, state)
        return plus(state, spread(b_buf[k]))

    def level_chunk(n, state):
        for i in range(CHUNK):
            await_b(1 + n * CHUNK + i)
        for i in range(CHUNK):
            state = level_turn(1 + n * CHUNK + i, state)
        return state

    coarse_start, coarse_initial = evolve(2, group_start, start)
    opens = group == 0
    await_b(0)
    opening = tuple(
        jnp.where(opens, a, b) for a, b in zip(relaxed_zero, level_turn(0, group_start))
    )
    closing = lax.fori_loop(0, (GROUP - 1) // CHUNK, level_chunk, opening)
    e_buf[group] = join(minus(closing, coarse_start))

    def e_copy(other):
        return remote(e_buf.at[group], e_buf.at[group], send_e.at[other], recv_e.at[group], other * GROUP + member)

    def start_e(other, carry):
        e_copy(other).start()
        return carry

    lax.fori_loop(group + 1, groups, start_e, 0)

    def await_e(other):
        remote(e_buf.at[other], e_buf.at[other], send_e.at[0], recv_e.at[other], me).wait_recv()

    def coarse_turn(other, before):
        await_e(other)
        (image,) = evolve(2, before)
        return plus(image, spread(e_buf[other]))

    @pl.when(group > 0)
    def _():
        await_e(0)

    first_coarse = plus(coarse_initial, spread(e_buf[0]))
    earlier = tuple(jnp.where(opens, a, b) for a, b in zip(start, first_coarse))
    earlier = lax.fori_loop(1, group, coarse_turn, earlier)

    def replay_chunk(n, state):
        for i in range(CHUNK):
            state = level_turn(n * CHUNK + i, state)
        return state

    chunks = member // CHUNK
    prior = lax.fori_loop(0, chunks, replay_chunk, earlier)
    prior = lax.fori_loop(chunks * CHUNK, member, level_turn, prior)
    (mine,) = evolve(2, earlier)
    mine = join(mine) + e_buf[group]
    (ending,) = evolve(1, prior)
    ending = join(ending) + b_buf[member]
    point = prior
    for i in range(STEPS_DEV - 1):
        (point,) = evolve(0, point)
        packed_ref[i] = join(point)
    last = member == GROUP - 1
    packed_ref[STEPS_DEV - 1] = jnp.where(last, mine, ending)
    packed_ref[STEPS_DEV + 1] = mine
    packed_ref[STEPS_DEV + 2] = jnp.where(last, ending - mine, 0.0)

    @pl.when(me >= 1)
    def _():
        remote(r_out, r_buf, send_r, recv_r, me).wait_recv()

    @pl.when(me >= 2)
    def _():
        remote(p_out, p_buf, send_p, recv_p, me).wait_recv()

    packed_ref[STEPS_DEV] = p_buf[...] - r_buf[...]

    @pl.when(jnp.logical_not(wraps))
    def _():
        over_peers(lambda i: b_copy(i).wait_send())

    @pl.when(relays)
    def _():
        over_peers(lambda i: b_relay(i).wait_send())

    @pl.when(jnp.logical_and(relays, first_wrap))
    def _():
        over_peers(lambda i: s_relay(i).wait_send())

    @pl.when(jnp.logical_and(forwards, first_wrap))
    def _():
        s_forward.wait_send()

    @pl.when(forwards)
    def _():
        b_forward.wait_send()

    @pl.when(me + 2 < devices)
    def _():
        p_copy.wait_send()

    @pl.when(me + 1 < devices)
    def _():
        r_copy.wait_send()

    def end_e(other, carry):
        e_copy(other).wait_send()
        return carry

    lax.fori_loop(group + 1, groups, end_e, 0)


def unpack(packed_ref, traj_ref, resid_ref, coarse_ref, defect_ref):
    cols = packed_ref.shape[2] // 2
    places = [(traj_ref, i) for i in range(STEPS_DEV)] + [(resid_ref, 0), (coarse_ref, 0), (defect_ref, 0)]
    for i, (ref, index) in enumerate(places):
        ref[index, 0] = packed_ref[i, :, :cols]
        ref[index, 1] = packed_ref[i, :, cols:]


assert (GROUP - 1) % CHUNK == 0


def shards(devices, initial, coarse_guess, feed_rate, kill_rate):
    rows, cols = initial.shape[1:]
    groups = devices // GROUP
    steps = (interval_time / STEPS_DEV, interval_time, interval_time * GROUP)
    tables = []
    for step in steps:
        tables += [jnp.asarray(table) for table in solve_tables(rows, cols, step)]
    state = (rows, 2 * cols)
    block = (1,) + initial.shape
    dma = pltpu.SemaphoreType.DMA
    whole = pl.BlockSpec(memory_space=pltpu.VMEM)
    buffer = pltpu.VMEM(state, jnp.float32)
    packed = pl.pallas_call(
        functools.partial(kernel, devices, (rows, cols)),
        out_shape=jax.ShapeDtypeStruct((STEPS_DEV + 3,) + state, jnp.float32),
        in_specs=[whole] * (4 + len(tables)),
        out_specs=whole,
        scratch_shapes=[
            pltpu.VMEM((9,) + state, jnp.float32),
            pltpu.VMEM((GROUP,) + state, jnp.float32),
            buffer,
            buffer,
            buffer,
            pltpu.VMEM((groups,) + state, jnp.float32),
        ]
        + [buffer] * 3
        + [dma((GROUP,)), dma((GROUP,)), dma((GROUP,))]
        + [dma] * 5
        + [dma((groups,)), dma((groups,)), dma, dma],
        compiler_params=pltpu.CompilerParams(collective_id=0, has_side_effects=True),
    )(initial, coarse_guess, feed_rate, kill_rate, *tables)
    return pl.pallas_call(
        unpack,
        out_shape=[
            jax.ShapeDtypeStruct((STEPS_DEV,) + initial.shape, jnp.float32),
            jax.ShapeDtypeStruct(block, jnp.float32),
            jax.ShapeDtypeStruct(block, jnp.float32),
            jax.ShapeDtypeStruct(block, jnp.float32),
        ],
        in_specs=[whole],
        out_specs=[whole] * 4,
    )(packed)


def solution(mesh):
    spread = P("tm", None, None, None)
    return jax.shard_map(
        functools.partial(shards, mesh.shape["tm"]),
        mesh=mesh,
        in_specs=(P(), spread, P(), P()),
        out_specs=(spread, spread, spread, spread),
        check_vma=False,
    )
```
